128 devices in a mesh: gx: 8 (over z, core), gy: 16 (over y, x).
Axes of the slice: x: 4, y: 4, z: 4, core: 2. Of those that a mesh axis runs over, the one named last changes fastest.
Arguments:
- fine_rhs: float32 [8, 16, 4, 32, 1024], P('gx', 'gy'), may hold values from -6 to 6
- fine_beta: float32 [8, 16, 4, 32, 1024], P('gx', 'gy'), may hold values from 0.5 to 5
- base_rhs: float32 [128, 256, 128], P('gx', 'gy'), may hold values from -6 to 6
- base_beta: float32 [128, 256, 128], P('gx', 'gy'), may hold values from 0.5 to 5
- slot_site: int32 [8, 16, 4], P('gx', 'gy'), may hold values from 0 to 7, as said below
- ghost_list: int32 [8, 16, 4, 6], P('gx', 'gy'), may hold values from -1 to 3, as said below
- box_count: int32 [8, 16], P('gx', 'gy'), may hold values from 1 to 4, as said below
Outputs:
- fine_solution: float32 [8, 16, 4, 32, 1024], P('gx', 'gy')
- base_solution: float32 [128, 256, 128], P('gx', 'gy')
The draws below stay inside these ranges and needn't reach their ends.
Inputs may be any that keep to these rules, and one draw needn't show every extreme that they name: `slot_site`: the slots of one column name distinct sites. `box_count`: some column holds exactly 4 live boxes in every draw. `ghost_list`: for a live slot, entry d is the slot of the live box at the adjacent site across face d (same site in the column beside it for x and y faces, the site below or above in the same column for z faces), or -1 if there is none; all entries of slots that are not live are -1.
All inputs are finite; a program needn't handle non-finite values.
Results may differ from the reference program's by a relative error of at most 0.0003.
Values sent between devices are 32-bit elements; how exact they have to be, the bound alone decides.
A program may use at most 128 MiB of HBM per device.

```python
import math
import jax
import jax.numpy as jnp
from jax import lax

CC = 16
NZC = 128
CYCLES = 2
SWEEPS = 6
F = 32
NS = 8
CAP = 4
COLX = 8
COLY = 16
NX = 128
NY = 256


def layout(base_key):
    base_key = jax.random.fold_in(base_key, 11)
    key_one, key_two, key_three, key_four, key_five = jax.random.split(base_key, 5)
    first_draw = jax.random.randint(key_one, (COLX, COLY), 0, CAP)
    second_draw = jax.random.randint(key_two, (COLX, COLY), 0, CAP)
    counts = jnp.minimum(CAP, CAP // 4 + 1 + first_draw * second_draw // (CAP - 1))
    full_column = jax.random.randint(key_three, (), 0, COLX * COLY)
    flat_counts = jnp.where(jnp.arange(COLX * COLY) == full_column, CAP, counts.reshape(-1))
    counts = flat_counts.reshape(COLX, COLY).astype(jnp.int32)
    shared = jax.random.randint(key_four, (NS,), 0, NS)
    local_part = jax.random.randint(key_five, (COLX, COLY, NS), 0, NS)
    scores = (2 * shared[None, None, :] + local_part) * NS + jnp.arange(NS)[None, None, :]
    order = jnp.argsort(scores, axis=-1).astype(jnp.int32)
    sites = order[..., :CAP]
    slot_ids = jnp.arange(CAP, dtype=jnp.int32)
    live_slots = slot_ids[None, None, :] < counts[..., None]
    matches = (sites[..., None, :] == jnp.arange(NS, dtype=jnp.int32)[None, None, :, None]) & live_slots[..., None, :]
    occupant = (jnp.sum(jnp.where(matches, slot_ids + 1, 0), axis=-1) - 1).astype(jnp.int32)
    empty_x = jnp.full((1, COLY, NS), -1, jnp.int32)
    empty_y = jnp.full((COLX, 1, NS), -1, jnp.int32)
    empty_z = jnp.full((COLX, COLY, 1), -1, jnp.int32)
    west_table = jnp.concatenate([empty_x, occupant[:-1]], axis=0)
    east_table = jnp.concatenate([occupant[1:], empty_x], axis=0)
    south_table = jnp.concatenate([empty_y, occupant[:, :-1]], axis=1)
    north_table = jnp.concatenate([occupant[:, 1:], empty_y], axis=1)
    lower_table = jnp.concatenate([empty_z, occupant[..., :-1]], axis=2)
    upper_table = jnp.concatenate([occupant[..., 1:], empty_z], axis=2)

    def at_sites(table):
        return jnp.take_along_axis(table, sites, axis=2)
    links = jnp.stack([at_sites(west_table), at_sites(east_table), at_sites(south_table), at_sites(north_table), at_sites(lower_table), at_sites(upper_table)], axis=-1)
    links = jnp.where(live_slots[..., None], links, -1).astype(jnp.int32)
    return (sites.astype(jnp.int32), links, counts)


def draw_slot_site(key, part):
    return layout(key)[0]


def draw_ghost_list(key, part):
    return layout(key)[1]


def draw_box_count(key, part):
    return layout(key)[2]


def steps_of(own_key, dims, cuts, least, high):
    factor_of = 1.0
    for axis_at, shards_of in cuts:
        steps = jax.random.uniform(jax.random.fold_in(jax.random.fold_in(own_key, 6), axis_at), (shards_of,), jnp.float32, least / len(cuts), high / len(cuts))
        factor_of = factor_of * jnp.repeat(jnp.exp(steps), dims[axis_at] // shards_of).reshape((-1,) + (1,) * (len(dims) - 1 - axis_at))
    return factor_of


def bell_draw(key, shape, scale, reach, cuts=(), held_as=jnp.bfloat16):
    factor_of = steps_of(key, shape, cuts, -0.22, 0.18) if cuts else 1.0
    drawn = jax.random.normal(key, shape, jnp.float32) * scale * factor_of
    return jnp.minimum(jnp.maximum(drawn, -reach), reach).astype(held_as)


def setup_inputs(seed: int = 0) -> dict:
    keys = jax.random.split(jax.random.key(seed), 8)
    fine_rhs = bell_draw(keys[0], (COLX, COLY, CAP, F, F * F), 1.0, 6.0, ((0, 8), (1, 16)), jnp.float32)
    fine_beta = jnp.clip(jnp.exp(math.log(5.0) - 2.3025851 * jax.random.uniform(keys[1], (COLX, COLY, CAP, F, F * F), jnp.float32) ** steps_of(keys[1], (COLX, COLY, CAP, F, F * F), ((0, 8), (1, 16)), -0.2, 0.2)), 0.5, 5.0)
    base_rhs = bell_draw(keys[2], (NX, NY, NZC), 1.0, 6.0, ((0, 8), (1, 16)), jnp.float32)
    base_beta = jnp.clip(jnp.exp(math.log(5.0) - 2.3025851 * jax.random.uniform(keys[3], (NX, NY, NZC), jnp.float32) ** steps_of(keys[3], (NX, NY, NZC), ((0, 8), (1, 16)), -0.2, 0.2)), 0.5, 5.0)
    slot_site = draw_slot_site(jax.random.fold_in(keys[7], 71), 0)
    ghost_list = draw_ghost_list(jax.random.fold_in(keys[7], 71), 0)
    box_count = draw_box_count(jax.random.fold_in(keys[7], 71), 0)
    return {"fine_rhs": fine_rhs, "fine_beta": fine_beta, "base_rhs": base_rhs, "base_beta": base_beta, "slot_site": slot_site, "ghost_list": ghost_list, "box_count": box_count}


damping = 2.0 / 3.0


def upsample(values, axis_list):
    for which_axis in axis_list:
        values = jnp.repeat(values, 2, axis=which_axis)
    return values


def shrink(values):
    size_x, size_y, size_z = values.shape
    blocks = values.reshape(size_x // 2, 2, size_y // 2, 2, size_z // 2, 2)
    return jnp.sum(blocks, axis=(1, 3, 5)) * 0.125


def level_apply(field, padded, coeffs, factor):
    nearby = padded[2:, 1:-1, 1:-1] + padded[:-2, 1:-1, 1:-1]
    nearby = nearby + padded[1:-1, 2:, 1:-1] + padded[1:-1, :-2, 1:-1]
    nearby = nearby + padded[1:-1, 1:-1, 2:] + padded[1:-1, 1:-1, :-2]
    return coeffs * factor * (6.0 * field - nearby)


def coarse_ghosts(halo_box, box_sites, extent):
    site_total = (halo_box.shape[2] - 2) // extent

    def from_plane(face_plane):
        slabs = jnp.take(face_plane.reshape(extent, site_total, extent), box_sites, axis=1)
        slabs = upsample(jnp.transpose(slabs, (1, 0, 2)), (1, 2))
        return slabs.reshape(slabs.shape[0], -1)

    column = halo_box[1:-1, 1:-1, :]

    def from_layer(layer_index):
        slabs = jnp.take(column, layer_index, axis=2)
        slabs = upsample(jnp.transpose(slabs, (2, 0, 1)), (1, 2))
        return slabs.reshape(slabs.shape[0], -1)

    return (from_plane(halo_box[0, 1:-1, 1:-1]), from_plane(halo_box[-1, 1:-1, 1:-1]),
            from_plane(halo_box[1:-1, 0, 1:-1]), from_plane(halo_box[1:-1, -1, 1:-1]),
            from_layer(box_sites * extent), from_layer((box_sites + 1) * extent + 1))


def fine_faces(field):
    slot_total, fine_edge, face_area = field.shape
    return (field[:, 0, :], field[:, -1, :],
            field[:, :, :fine_edge].reshape(slot_total, face_area),
            field[:, :, face_area - fine_edge:].reshape(slot_total, face_area),
            field[:, :, 0::fine_edge].reshape(slot_total, face_area),
            field[:, :, fine_edge - 1::fine_edge].reshape(slot_total, face_area))


def choose(received, link_index, fallback):
    picked = jnp.take(received, jnp.maximum(link_index, 0), axis=0)
    return jnp.where((link_index >= 0)[:, None], picked, fallback)


def assemble(face_set, from_west, from_east, from_south, from_north, coarse, link_table):
    return (choose(from_west, link_table[:, 0], coarse[0]), choose(from_east, link_table[:, 1], coarse[1]),
            choose(from_south, link_table[:, 2], coarse[2]), choose(from_north, link_table[:, 3], coarse[3]),
            choose(face_set[5], link_table[:, 4], coarse[4]), choose(face_set[4], link_table[:, 5], coarse[5]))


def apply_fine(field, coeffs, layers):
    slot_total, fine_edge, face_area = field.shape
    depth_pos = jnp.arange(face_area) % fine_edge
    west_side = jnp.concatenate([layers[0][:, None, :], field[:, :-1, :]], axis=1)
    east_side = jnp.concatenate([field[:, 1:, :], layers[1][:, None, :]], axis=1)
    south_side = jnp.concatenate([layers[2].reshape(slot_total, fine_edge, fine_edge), field[:, :, :face_area - fine_edge]], axis=2)
    north_side = jnp.concatenate([field[:, :, fine_edge:], layers[3].reshape(slot_total, fine_edge, fine_edge)], axis=2)
    zero_slab = jnp.zeros((slot_total, fine_edge, 1), field.dtype)
    lower_side = jnp.where(depth_pos == 0,
                           jnp.repeat(layers[4].reshape(slot_total, fine_edge, fine_edge), fine_edge, axis=2),
                           jnp.concatenate([zero_slab, field[:, :, :-1]], axis=2))
    upper_side = jnp.where(depth_pos == fine_edge - 1,
                           jnp.repeat(layers[5].reshape(slot_total, fine_edge, fine_edge), fine_edge, axis=2),
                           jnp.concatenate([field[:, :, 1:], zero_slab], axis=2))
    return coeffs * (6.0 * field - (west_side + east_side + south_side + north_side + lower_side + upper_side))


def restrict_fine(field):
    slot_total, fine_edge, face_area = field.shape
    half_edge = fine_edge // 2
    blocks = field.reshape(slot_total, half_edge, 2, half_edge, 2, half_edge, 2)
    return jnp.sum(blocks, axis=(2, 4, 6)) * 0.125


def insert_blocks(coarse, blocks, box_sites, live_slots):
    extent = coarse.shape[0]
    site_total = coarse.shape[2] // extent
    slot_ids = jnp.arange(blocks.shape[0], dtype=jnp.int32)
    matches = (box_sites[None, :] == jnp.arange(site_total, dtype=jnp.int32)[:, None]) & live_slots[None, :]
    owner = (jnp.sum(jnp.where(matches, slot_ids[None, :] + 1, 0), axis=1) - 1).astype(jnp.int32)
    picked = jnp.transpose(jnp.take(blocks, jnp.maximum(owner, 0), axis=0), (1, 2, 0, 3))
    stacked = coarse.reshape(extent, extent, site_total, extent)
    merged = jnp.where((owner >= 0)[None, None, :, None], picked, stacked)
    return merged.reshape(coarse.shape)


def prolong_fine(coarse, box_sites):
    extent = coarse.shape[0]
    site_total = coarse.shape[2] // extent
    slabs = jnp.take(coarse.reshape(extent, extent, site_total, extent), box_sites, axis=2)
    slabs = upsample(jnp.transpose(slabs, (2, 0, 1, 3)), (1, 2, 3))
    return slabs.reshape(slabs.shape[0], 2 * extent, -1)


def per_column(function):
    return jax.vmap(jax.vmap(function))


def reference(fine_rhs, fine_beta, base_rhs, base_beta, slot_site, ghost_list, box_count):
    column_total = COLX * COLY
    live_slots = jnp.arange(CAP, dtype=jnp.int32)[None, None, :] < box_count[:, :, None]
    keep_mask = live_slots.astype(jnp.float32)[..., None, None]
    coeff_levels = [base_beta]
    for level_index in range(3):
        coeff_levels.append(shrink(coeff_levels[-1]))
    factor_levels = [0.25 ** (level_index + 1) for level_index in range(4)]

    def to_columns(values):
        return values.reshape(COLX, CC, COLY, CC, NZC).transpose(0, 2, 1, 3, 4)

    def from_columns(values):
        return values.transpose(0, 2, 1, 3, 4).reshape(NX, NY, NZC)

    def windows(base_field):
        padded = jnp.pad(base_field, 1)
        starts_x = jnp.arange(COLX, dtype=jnp.int32) * CC
        starts_y = jnp.arange(COLY, dtype=jnp.int32) * CC
        anchor = jnp.zeros((), jnp.int32)

        def window_at(start_x, start_y):
            return lax.dynamic_slice(padded, (start_x, start_y, anchor), (CC + 2, CC + 2, NZC + 2))

        return jax.vmap(lambda start_x: jax.vmap(lambda start_y: window_at(start_x, start_y))(starts_y))(starts_x)

    def ghost_layers(fine_field, halo_boxes):
        face_set = per_column(fine_faces)(fine_field)
        coarse = per_column(lambda halo_box, box_sites: coarse_ghosts(halo_box, box_sites, CC))(halo_boxes, slot_site)
        blank_row = jnp.zeros_like(face_set[0][:1])
        from_west = jnp.concatenate([blank_row, face_set[1][:-1]], axis=0)
        from_east = jnp.concatenate([face_set[0][1:], blank_row], axis=0)
        blank_col = jnp.zeros_like(face_set[0][:, :1])
        from_south = jnp.concatenate([blank_col, face_set[3][:, :-1]], axis=1)
        from_north = jnp.concatenate([face_set[2][:, 1:], blank_col], axis=1)
        return per_column(assemble)(face_set, from_west, from_east, from_south, from_north, coarse, ghost_list)

    def by_column(function, arrays):
        flat = jax.tree.map(lambda values: values.reshape((column_total,) + values.shape[2:]), arrays)
        result = lax.map(lambda packed: function(*packed), flat)
        return result.reshape((COLX, COLY) + result.shape[1:])

    def smooth_column(field, coeffs, rhs_values, layers, keep):
        return (field + damping * (rhs_values - apply_fine(field, coeffs, layers)) / (6.0 * coeffs)) * keep

    def leftover_column(field, coeffs, rhs_values, layers):
        return rhs_values - apply_fine(field, coeffs, layers)

    def smooth(fine_field, base_field):
        layers = ghost_layers(fine_field, windows(base_field))
        return by_column(smooth_column, (fine_field, fine_beta, fine_rhs, layers, keep_mask))

    def insert_all(base_values, fine_values):
        blocks = per_column(restrict_fine)(fine_values)
        merged = per_column(insert_blocks)(to_columns(base_values), blocks, slot_site, live_slots)
        return from_columns(merged)

    def multigrid(residual, level_index):
        coeffs = coeff_levels[level_index]
        factor = factor_levels[level_index]
        diagonal = 6.0 * coeffs * factor
        correction = damping * residual / diagonal
        if level_index == 3:
            for sweep_index in range(SWEEPS - 1):
                correction = correction + damping * (residual - level_apply(correction, jnp.pad(correction, 1), coeffs, factor)) / diagonal
            return correction
        leftover_part = residual - level_apply(correction, jnp.pad(correction, 1), coeffs, factor)
        correction = correction + upsample(multigrid(shrink(leftover_part), level_index + 1), (0, 1, 2))
        return correction + damping * (residual - level_apply(correction, jnp.pad(correction, 1), coeffs, factor)) / diagonal

    fine_field = jnp.zeros_like(fine_rhs)
    base_field = jnp.zeros_like(base_rhs)
    for cycle_index in range(CYCLES):
        halo_boxes = windows(base_field)
        fine_field = by_column(smooth_column, (fine_field, fine_beta, fine_rhs, ghost_layers(fine_field, halo_boxes), keep_mask))
        fine_left = by_column(leftover_column, (fine_field, fine_beta, fine_rhs, ghost_layers(fine_field, halo_boxes)))
        base_left = base_rhs - level_apply(base_field, jnp.pad(base_field, 1), coeff_levels[0], factor_levels[0])
        base_left = insert_all(base_left, fine_left)
        correction = multigrid(base_left, 0)
        base_field = base_field + correction
        fine_field = (fine_field + per_column(prolong_fine)(to_columns(correction), slot_site)) * keep_mask
        fine_field = smooth(fine_field, base_field)
        base_field = insert_all(base_field, fine_field)
    return fine_field, base_field
```

```python
import jax
import jax.numpy as jnp
from jax import lax
from jax.experimental import pallas as pl
from jax.experimental.pallas import tpu as pltpu
from jax.sharding import PartitionSpec as P

CYCLES = 2
SWEEPS = 6
MESH = pl.DeviceIdType.MESH
F32 = jnp.float32

S0, O0 = 24, 4
S1, O1 = 24, 8
S2, O2 = 8, 2

DIRS = ((-1, 0), (1, 0), (0, -1), (0, 1), (-1, -1), (-1, 1), (1, -1), (1, 1))
REACH = (-3, -2, -1, 1, 2, 3)
PARTNERS = DIRS + tuple((0, k) for k in (-3, -2, 2, 3)) + tuple((k, 0) for k in (-3, -2, 2, 3))

SEM_COUNT = 8 + 4 + 2 * (4 + 8 + 8 + 6 + 6)


def roll(value, shift, axis):
    return pltpu.roll(value, shift % value.shape[axis], axis)


def tile(value, count):
    return value if count == 1 else jnp.concatenate([value] * count, axis=0)


def pick(value, index):
    parts = [
        jnp.take_along_axis(value[k : k + 8], index, axis=1, mode="promise_in_bounds")
        for k in range(0, value.shape[0], 8)
    ]
    return parts[0] if len(parts) == 1 else jnp.concatenate(parts, axis=0)


def kernel(
    nx,
    ny,
    site_ref,
    link_ref,
    count_ref,
    frhs_ref,
    fbeta_ref,
    brhs_ref,
    bbeta_ref,
    fout_ref,
    bout_ref,
    FA,
    FB,
    G,
    BT,
    PC,
    CGZ,
    T,
    GX,
    CB,
    B0,
    BR,
    C0,
    W0,
    P0,
    E0,
    T0,
    C1,
    W1,
    P1,
    E1,
    U1,
    T1,
    C2,
    W2,
    P2,
    E2,
    T2,
    W3,
    SP,
    RP,
    SA,
    RA,
    SB,
    RB,
    SC,
    SCC,
    RC,
    RCC,
    SD,
    RD,
    SW,
    RW,
    SX,
    RX,
    send_sem,
    recv_sem,
):
    gx = lax.axis_index("gx")
    gy = lax.axis_index("gy")
    counter = [0]
    pending = []

    def inside(dx, dy):
        conds = []
        if dx < 0:
            conds.append(gx >= -dx)
        if dx > 0:
            conds.append(gx < nx - dx)
        if dy < 0:
            conds.append(gy >= -dy)
        if dy > 0:
            conds.append(gy < ny - dy)
        out = conds[0]
        for cond in conds[1:]:
            out = jnp.logical_and(out, cond)
        return out

    def start(messages):
        sent = []
        for dx, dy, source, target in messages:
            k = counter[0]
            counter[0] += 1

            def copy(dx=dx, dy=dy, source=source, target=target, k=k):
                return pltpu.make_async_remote_copy(
                    src_ref=source,
                    dst_ref=target,
                    send_sem=send_sem.at[k],
                    recv_sem=recv_sem.at[k],
                    device_id=(gx + dx, gy + dy),
                    device_id_type=MESH,
                )

            pl.when(inside(dx, dy))(lambda copy=copy: copy().start())
            sent.append((dx, dy, copy))
        pending.extend(sent)
        return sent

    def finish(sent):
        for dx, dy, copy in sent:
            pl.when(inside(-dx, -dy))(lambda copy=copy: copy().wait_recv())

    for ref in (B0, BR, C0, W0, P0, E0, C1, P1, E1, U1, FA, FB, GX, CB, SCC, RX):
        ref[...] = jnp.zeros(ref.shape, F32)
    for ref in (RP, RA, RB, RC, RCC, RD, RW):
        ref[...] = jnp.zeros(ref.shape, F32)

    barrier = pltpu.get_barrier_semaphore()
    total = jnp.int32(0)
    for dx, dy in PARTNERS:
        there = inside(dx, dy)

        def greet(dx=dx, dy=dy):
            pl.semaphore_signal(barrier, inc=1, device_id=(gx + dx, gy + dy), device_id_type=MESH)

        pl.when(there)(greet)
        total = total + there.astype(jnp.int32)

    lane = lax.broadcasted_iota(jnp.int32, (8, 128), 1)
    row8 = lax.broadcasted_iota(jnp.int32, (8, 128), 0)
    slot = lane >> 5
    zf = lane & 31
    sites = [site_ref[0, 0, s] for s in range(4)]
    count = count_ref[0, 0]

    def by_slot(values):
        out = jnp.full((8, 128), values[3], jnp.int32)
        for s in (2, 1, 0):
            out = jnp.where(slot == s, values[s], out)
        return out

    site_v = by_slot(sites)
    links = [by_slot([link_ref[0, 0, s, d] for s in range(4)]) for d in range(6)]
    keep8 = jnp.where(slot < count, 1.0, 0.0).astype(F32)
    index_low = jnp.where(zf == 0, jnp.maximum(links[4], 0) * 32 + 31, jnp.maximum(lane - 1, 0))
    index_high = jnp.where(zf == 31, jnp.maximum(links[5], 0) * 32, jnp.minimum(lane + 1, 127))
    mask_low = jnp.where((zf > 0) | (links[4] >= 0), 1.0, 0.0).astype(F32)
    mask_high = jnp.where((zf < 31) | (links[5] >= 0), 1.0, 0.0).astype(F32)
    index_p = site_v * 16 + (zf >> 1)
    index_cz = jnp.where(zf < 16, jnp.maximum(site_v * 16 - 1, 0), jnp.minimum(site_v * 16 + 16, 127))
    mask_cz = jnp.where(
        ((zf == 0) & (links[4] < 0) & (site_v > 0)) | ((zf == 31) & (links[5] < 0) & (site_v < 7)), 1.0, 0.0
    ).astype(F32)
    index_g = [jnp.maximum(links[d], 0) * 32 + zf for d in range(4)]
    mask_g = [jnp.where(links[d] >= 0, 1.0, 0.0).astype(F32) for d in range(4)]
    index_in = jnp.zeros((8, 128), jnp.int32)
    mask_in = jnp.zeros((8, 128), F32)
    for s in range(4):
        held = ((lane >> 4) == sites[s]) & (count > s)
        index_in = jnp.where(held, s * 32 + 2 * (lane & 15), index_in)
        mask_in = jnp.where(held, 1.0, mask_in)
    keep32 = tile(keep8, 4)
    mask_low32 = tile(mask_low, 4)
    mask_high32 = tile(mask_high, 4)
    mask_in16 = tile(mask_in, 2)
    row32 = lax.broadcasted_iota(jnp.int32, (32, 128), 0)
    first32 = jnp.where(row32 == 0, 1.0, 0.0).astype(F32)
    last32 = jnp.where(row32 == 31, 1.0, 0.0).astype(F32)

    lane32 = lax.broadcasted_iota(jnp.int32, (32, 128), 1)
    bit0 = ((lane32 >> 5) & 1) == 0
    bit1 = ((lane32 >> 6) & 1) == 0

    def swap(a, b, bit, shift):
        return jnp.where(bit, a, roll(b, shift, 1)), jnp.where(bit, roll(a, -shift, 1), b)

    def exchange_chunks(parts):
        a, b = swap(parts[0], parts[1], bit0, 32)
        c, d = swap(parts[2], parts[3], bit0, 32)
        a, c = swap(a, c, bit1, 64)
        b, d = swap(b, d, bit1, 64)
        return a, b, c, d

    def load_fine(j, _):
        lanes = pl.ds(pl.multiple_of(j * 128, 128), 128)
        betas = exchange_chunks([fbeta_ref[0, 0, s, :, lanes] for s in range(4)])
        values = exchange_chunks([frhs_ref[0, 0, s, :, lanes] for s in range(4)])
        for k in range(4):
            at = pl.multiple_of((4 * j + k) * 32, 32)
            g = values[k] / (9.0 * betas[k])
            BT[pl.ds(at, 32), :] = betas[k]
            G[pl.ds(at, 32), :] = g
            FA[pl.ds(at + 32, 32), :] = g * keep32
        return 0

    lax.fori_loop(0, 8, load_fine, 0)

    def pack_faces(stage):
        stage[0, 0:32, :] = FA[pl.ds(32, 32, stride=32), :]
        stage[1, 0:32, :] = FA[pl.ds(63, 32, stride=32), :]
        stage[2, 0:32, :] = FA[32:64, :]
        stage[3, 0:32, :] = FA[32 * 32 : 33 * 32, :]

    def send_faces(stage, inbox):
        return start([(*DIRS[d], stage.at[d], inbox.at[d]) for d in range(4)])

    pl.semaphore_wait(barrier, total)
    pack_faces(SB.at[0])
    wait_b = send_faces(SB.at[0], RB.at[0])

    lane8 = lane

    def pair(value, shift):
        wide = lax.broadcasted_iota(jnp.int32, value.shape, 1)
        return value + jnp.where((wide & shift) == 0, roll(value, -shift, 1), roll(value, shift, 1))

    for y in range(16):
        beta = bbeta_ref[pl.ds(y, 16, stride=16), :]
        c = beta * 0.25
        at = (y + 2) * S0 + O0
        C0[at : at + 16, :] = c
        W0[at : at + 16, :] = 1.0 / (9.0 * c)
        BR[at : at + 16, :] = brhs_ref[pl.ds(y, 16, stride=16), :]

    def restrict0(values, y):
        t = pair(values(2 + 2 * y) + values(3 + 2 * y), 1)
        T0[y * S0 : (y + 1) * S0, :] = t
        return (T0[pl.ds(y * S0 + O0, 8, stride=2), :] + T0[pl.ds(y * S0 + O0 + 1, 8, stride=2), :]) * 0.125

    def restrict1(values, y):
        t = pair(values(1 + 2 * y) + values(2 + 2 * y), 2)
        T1[y * S1 : (y + 1) * S1, :] = t
        return (T1[pl.ds(y * S1 + 4, 8, stride=2), :] + T1[pl.ds(y * S1 + 5, 8, stride=2), :]) * 0.125

    def restrict2(values, y):
        t = pair(values(2 + 2 * y) + values(3 + 2 * y), 4)
        T2[y * S2 : (y + 1) * S2, :] = t
        return (T2[pl.ds(y * S2, 4, stride=2), :] + T2[pl.ds(y * S2 + 1, 4, stride=2), :]) * 0.125

    for y in range(8):
        c = restrict0(lambda p: C0[p * S0 : (p + 1) * S0, :], y) * 0.25
        C1[(y + 5) * S1 + O1 : (y + 5) * S1 + O1 + 8, :] = c
        W1[y * 8 : y * 8 + 8, :] = 1.0 / (9.0 * c)

    def send_level1(ref, stage, inbox):
        for k in range(5):
            stage[0, k * 8 : k * 8 + 8, :] = ref[pl.ds(5 * S1 + O1 + k, 8, stride=S1), :]
            stage[1, k * 8 : k * 8 + 8, :] = ref[pl.ds(5 * S1 + O1 + 3 + k, 8, stride=S1), :]
            stage[2, k * 8 : k * 8 + 8, :] = ref[(5 + k) * S1 + O1 : (5 + k) * S1 + O1 + 8, :]
            stage[3, k * 8 : k * 8 + 8, :] = ref[(8 + k) * S1 + O1 : (8 + k) * S1 + O1 + 8, :]
        source = (0, 1, 2, 3, 2, 3, 2, 3)
        return start([(*DIRS[d], stage.at[source[d]], inbox.at[d]) for d in range(8)])

    def unpack_level1(ref, inbox):
        for k in range(5):
            part = slice(k * 8, k * 8 + 8)
            ref[pl.ds(5 * S1 + 16 + k, 8, stride=S1), :] = inbox[0, part, :]
            ref[pl.ds(5 * S1 + 3 + k, 8, stride=S1), :] = inbox[1, part, :]
            low, high = k * S1, (13 + k) * S1
            ref[high + 8 : high + 16, :] = inbox[2, part, :]
            ref[low + 8 : low + 16, :] = inbox[3, part, :]
            ref[high + 16 : high + 24, :] = inbox[4, part, :]
            ref[low + 16 : low + 24, :] = inbox[5, part, :]
            ref[high : high + 8, :] = inbox[6, part, :]
            ref[low : low + 8, :] = inbox[7, part, :]

    wait_p = send_level1(C1, SP, RP)

    def neighbours(ref, plane, rows, shift):
        c = ref[plane * rows : (plane + 1) * rows, :]
        wide = lax.broadcasted_iota(jnp.int32, (rows, 128), 1)
        total = ref[(plane + 1) * rows : (plane + 2) * rows, :] + ref[(plane - 1) * rows : plane * rows, :]
        total = total + (roll(c, 1, 0) + roll(c, -1, 0))
        low = jnp.where(wide >= shift, roll(c, shift, 1), 0.0)
        high = jnp.where(wide < 128 - shift, roll(c, -shift, 1), 0.0)
        return c, total + (low + high)

    def row_mask(rows, first, extent, count):
        at = lax.broadcasted_iota(jnp.int32, (rows, 128), 0) - first + gx * extent
        return jnp.where((at >= 0) & (at < count), 1.0, 0.0).astype(F32)

    def plane_mask(y, extent, count):
        at = y + gy * extent
        return jnp.where((at >= 0) & (at < count), 1.0, 0.0).astype(F32)

    rows0 = row_mask(S0, O0, 16, nx * 16)
    rows1 = row_mask(S1, O1, 8, nx * 8)
    rows2 = row_mask(S2, O2, 4, nx * 4)

    def post(pre, field, plane, rows, shift, mask, scale):
        c, around = neighbours(field, plane, rows, shift)
        return pre[plane * rows : (plane + 1) * rows, :] + (mask * scale) * (c * (1.0 / 3.0) + around * (1.0 / 9.0))

    def fine_around(field, y, center):
        at = pl.multiple_of(y * 32, 32)
        total = field[pl.ds(at, 32), :] + field[pl.ds(at + 64, 32), :]
        low = jnp.broadcast_to(GX[0, pl.ds(y, 1), :], (32, 128))
        high = jnp.broadcast_to(GX[1, pl.ds(y, 1), :], (32, 128))
        total = total + jnp.where(first32 > 0, low, roll(center, 1, 0)) + jnp.where(last32 > 0, high, roll(center, -1, 0))
        total = total + (pick(center, index_low) * mask_low32 + pick(center, index_high) * mask_high32)
        return total + CGZ[pl.ds(pl.multiple_of((y >> 1) * 32, 32), 32), :]

    def restrict_fine(values, y):
        at = pl.multiple_of(y * 32, 32)
        T[pl.ds(at, 32), :] = values
        t = T[pl.ds(at, 16, stride=2), :] + T[pl.ds(at + 1, 16, stride=2), :]
        return pick(t + roll(t, -1, 1), index_in) * 0.125

    def double(ref, at, value):
        ref[pl.ds(at, value.shape[0], stride=2), :] = value
        ref[pl.ds(at + 1, value.shape[0], stride=2), :] = value

    def set_ghosts(inbox):
        GX[0, :, :] = pick(inbox[1, 0:32, :], index_g[0]) * tile(mask_g[0], 4) + CB[0:32, :]
        GX[1, :, :] = pick(inbox[0, 0:32, :], index_g[1]) * tile(mask_g[1], 4) + CB[32:64, :]
        FA[0:32, :] = pick(inbox[3, 0:32, :], index_g[2]) * tile(mask_g[2], 4) + CB[64:96, :]
        FA[33 * 32 : 34 * 32, :] = pick(inbox[2, 0:32, :], index_g[3]) * tile(mask_g[3], 4) + CB[96:128, :]

    def outer(ref, d):
        if d == 0:
            return ref[pl.ds(2 * S0 + O0 - 1, 16, stride=S0), :]
        if d == 1:
            return ref[pl.ds(2 * S0 + O0 + 16, 16, stride=S0), :]
        plane = 1 if d == 2 else 18
        return ref[plane * S0 + O0 : plane * S0 + O0 + 16, :]

    def coarse_z():
        for y in range(16):
            at = (y + 2) * S0 + O0
            double(CGZ, y * 32, pick(B0[at : at + 16, :], index_cz) * tile(mask_cz, 2))

    for cycle in range(CYCLES):
        if cycle == 0:
            CGZ[...] = jnp.zeros(CGZ.shape, F32)
        else:
            pack_faces(SA)
            SA[0, 32:48, :] = B0[pl.ds(2 * S0 + O0, 16, stride=S0), :]
            SA[1, 32:48, :] = B0[pl.ds(2 * S0 + O0 + 15, 16, stride=S0), :]
            SA[2, 32:48, :] = B0[2 * S0 + O0 : 2 * S0 + O0 + 16, :]
            SA[3, 32:48, :] = B0[17 * S0 + O0 : 17 * S0 + O0 + 16, :]
            wait_a = send_faces(SA, RA)
            coarse_z()
            finish(wait_a)
            B0[pl.ds(2 * S0 + O0 + 16, 16, stride=S0), :] = RA[0, 32:48, :]
            B0[pl.ds(2 * S0 + O0 - 1, 16, stride=S0), :] = RA[1, 32:48, :]
            B0[18 * S0 + O0 : 18 * S0 + O0 + 16, :] = RA[2, 32:48, :]
            B0[1 * S0 + O0 : 1 * S0 + O0 + 16, :] = RA[3, 32:48, :]
            for d in range(4):
                double(CB, d * 32, pick(outer(B0, d), index_p) * tile(1.0 - mask_g[d], 2))
            set_ghosts(RA)

            def first_sweep(y, _):
                at = pl.multiple_of(y * 32, 32)
                center = FA[pl.ds(at + 32, 32), :]
                around = fine_around(FA, y, center)
                FB[pl.ds(at + 32, 32), :] = keep32 * (
                    G[pl.ds(at, 32), :] + center * (1.0 / 3.0) + around * (1.0 / 9.0)
                )
                return 0

            lax.fori_loop(0, 32, first_sweep, 0, unroll=2)

            def copy_back(y, _):
                at = pl.ds(pl.multiple_of(y * 32 + 32, 32), 32)
                FA[at, :] = FB[at, :]
                return 0

            lax.fori_loop(0, 32, copy_back, 0, unroll=4)
            pack_faces(SB.at[cycle])
            wait_b = send_faces(SB.at[cycle], RB.at[cycle])

        if cycle == 0:
            for y in range(16):
                at = (y + 2) * S0
                P0[at : at + S0, :] = BR[at : at + S0, :]
        else:
            for y in range(16):
                at = (y + 2) * S0
                c, around = neighbours(B0, y + 2, S0, 1)
                P0[at : at + S0, :] = BR[at : at + S0, :] - C0[at : at + S0, :] * (6.0 * c - around)

        finish(wait_b)
        set_ghosts(RB.at[cycle])

        def residual(y, _):
            def one(k):
                at = pl.multiple_of(k * 32, 32)
                center = FA[pl.ds(at + 32, 32), :]
                around = fine_around(FA, k, center)
                return BT[pl.ds(at, 32), :] * (9.0 * G[pl.ds(at, 32), :] - 6.0 * center + around)

            both = one(2 * y) + one(2 * y + 1)
            T[pl.ds(pl.multiple_of(y * 32, 32), 32), :] = both
            return 0

        lax.fori_loop(0, 16, residual, 0)
        for y in range(16):
            t = T[pl.ds(y * 32, 16, stride=2), :] + T[pl.ds(y * 32 + 1, 16, stride=2), :]
            means = pick(t + roll(t, -1, 1), index_in) * 0.125
            at = (y + 2) * S0 + O0
            P0[at : at + 16, :] = jnp.where(mask_in16 > 0, means, P0[at : at + 16, :]) * W0[at : at + 16, :]

        stage, corner = SC.at[cycle], SCC.at[cycle]
        for k in range(2):
            part = slice(k * 16, k * 16 + 16)
            stage[0, part, :] = P0[pl.ds(2 * S0 + O0 + k, 16, stride=S0), :]
            stage[1, part, :] = P0[pl.ds(2 * S0 + O0 + 14 + k, 16, stride=S0), :]
            stage[2, part, :] = P0[(2 + k) * S0 + O0 : (2 + k) * S0 + O0 + 16, :]
            stage[3, part, :] = P0[(16 + k) * S0 + O0 : (16 + k) * S0 + O0 + 16, :]
            for d in range(4):
                dx, dy = DIRS[4 + d]
                at = ((2 if dy < 0 else 16) + k) * S0 + O0 + (0 if dx < 0 else 14)
                corner[d, 2 * k : 2 * k + 2, :] = P0[at : at + 2, :]
        inbox, corners = RC.at[cycle], RCC.at[cycle]
        wait_c = start(
            [(*DIRS[d], stage.at[d], inbox.at[d]) for d in range(4)]
            + [(*DIRS[4 + d], corner.at[d], corners.at[d]) for d in range(4)]
        )
        finish(wait_c)
        for k in range(2):
            part = slice(k * 16, k * 16 + 16)
            P0[pl.ds(2 * S0 + O0 + 16 + k, 16, stride=S0), :] = inbox[0, part, :]
            P0[pl.ds(2 * S0 + O0 - 2 + k, 16, stride=S0), :] = inbox[1, part, :]
            P0[(18 + k) * S0 + O0 : (18 + k) * S0 + O0 + 16, :] = inbox[2, part, :]
            P0[k * S0 + O0 : k * S0 + O0 + 16, :] = inbox[3, part, :]
            for d in range(4):
                dx, dy = DIRS[4 + d]
                at = ((18 if dy < 0 else 0) + k) * S0 + (O0 + 16 if dx < 0 else O0 - 2)
                P0[at : at + 2, :] = corners[d, 2 * k : 2 * k + 2, :]

        def left0(plane):
            c, around = neighbours(P0, plane, S0, 1)
            return C0[plane * S0 : (plane + 1) * S0, :] * (3.0 * c + around)

        for y in range(8):
            at = (y + 5) * S1 + O1
            P1[at : at + 8, :] = restrict0(left0, y) * W1[y * 8 : y * 8 + 8, :]
        wait_d = send_level1(P1, SD.at[cycle], RD.at[cycle])
        if cycle == 0:
            finish(wait_p)
            unpack_level1(C1, RP)
            for y in range(8):
                c = restrict1(lambda p: C1[p * S1 : (p + 1) * S1, :], y) * 0.25
                C2[y * 8 : y * 8 + 8, :] = c
                W2[y * 8 : y * 8 + 8, :] = jnp.where(c > 0, 1.0 / (9.0 * jnp.where(c > 0, c, 1.0)), 0.0)
            for y in range(2):
                c = restrict2(lambda p: C2[p * S2 : (p + 1) * S2, :], y) * 0.25
                W3[y * 4 : y * 4 + 4, :] = jnp.where(c > 0, 1.0 / (9.0 * jnp.where(c > 0, c, 1.0)), 0.0)
        finish(wait_d)
        unpack_level1(P1, RD.at[cycle])

        def left1(plane):
            c, around = neighbours(P1, plane, S1, 2)
            return C1[plane * S1 : (plane + 1) * S1, :] * (3.0 * c + around)

        for y in range(8):
            P2[y * 8 : y * 8 + 8, :] = restrict1(left1, y) * W2[y * 8 : y * 8 + 8, :]

        def left2(plane):
            c, around = neighbours(P2, plane, S2, 4)
            return C2[plane * S2 : (plane + 1) * S2, :] * (3.0 * c + around)

        mine = jnp.concatenate([restrict2(left2, y) for y in range(2)], axis=0) * W3[...]
        strip = SW.at[cycle]
        strip[...] = pick(mine, (lane8 & 15) * 8)
        wait_w = start([(0, k, strip, RW.at[cycle, 3 - k]) for k in REACH])
        finish(wait_w)
        joined = jnp.where((lane8 >> 4) == 3, strip[...], 0.0)
        for k in REACH:
            joined = jnp.where((lane8 >> 4) == 3 + k, RW[cycle, 3 + k, :, :], joined)
        SX[cycle, :, :] = joined
        wait_x = start([(k, 0, SX.at[cycle], RX.at[cycle, pl.ds((3 - k) * 8, 8)]) for k in REACH])
        RX[cycle, 24:32, :] = joined
        finish(wait_x)

        first = [[RX[cycle, pl.ds(y * 4 + 1 + x, 8, stride=8), :] for x in range(2)] for y in range(2)]
        col_x = gx + row8 - 3
        col_y = gy + (lane8 >> 4) - 3
        there = (col_x >= 0) & (col_x < nx) & (row8 < 7) & (col_y >= 0) & (col_y < ny) & (lane8 < 112)
        mask3 = jnp.where(there, 1.0, 0.0).astype(F32)
        e = first
        for sweep in range(SWEEPS - 1):
            new = [[None, None], [None, None]]
            for y in range(2):
                for x in range(2):
                    c, ex, ey = e[y][x], e[y][1 - x], e[1 - y][x]
                    around = ex + roll(ex, 1 if x == 0 else -1, 0) + ey + roll(ey, 16 if y == 0 else -16, 1)
                    around = around + jnp.where((lane8 & 15) > 0, roll(c, 1, 1), 0.0)
                    around = around + jnp.where((lane8 & 15) < 15, roll(c, -1, 1), 0.0)
                    new[y][x] = first[y][x] + mask3 * (c * (1.0 / 3.0) + around * (1.0 / 9.0))
            e = new

        from_one = jnp.where(row8 < 2, 2, 3)
        from_zero = jnp.where(row8 < 4, 3, 4)
        for k, (column, y) in enumerate(((2, 1), (3, 0), (3, 1), (4, 0))):
            lanes = column * 16 + (lane8 >> 3)
            zero, one = pick(e[y][0], lanes), pick(e[y][1], lanes)
            zero = jnp.take_along_axis(zero, from_zero, axis=0, mode="promise_in_bounds")
            one = jnp.take_along_axis(one, from_one, axis=0, mode="promise_in_bounds")
            up = jnp.where((row8 & 2) == 0, one, zero)
            for plane in (2 * k, 2 * k + 1):
                E2[plane * 8 : plane * 8 + 8, :] = P2[plane * 8 : plane * 8 + 8, :] + up
        for plane in range(1, 7):
            up = post(P2, E2, plane, S2, 4, rows2, plane_mask(plane - 2, 4, ny * 4))
            at = plane * S1
            double(U1, at + 4, up)
            for fine in (2 * plane + 1, 2 * plane + 2):
                E1[fine * S1 : (fine + 1) * S1, :] = P1[fine * S1 : (fine + 1) * S1, :] + U1[at : at + S1, :]
        for plane in range(4, 14):
            at = plane * S1
            U1[at : at + S1, :] = post(P1, E1, plane, S1, 2, rows1, plane_mask(plane - 5, 8, ny * 8))
            value = U1[at + 7 : at + 17, :]
            fine = 2 * (plane - 4)
            double(E0, fine * S0 + 2, value)
            up = E0[fine * S0 : (fine + 1) * S0, :]
            E0[(fine + 1) * S0 : (fine + 2) * S0, :] = up + P0[(fine + 1) * S0 : (fine + 2) * S0, :]
            E0[fine * S0 : (fine + 1) * S0, :] = up + P0[fine * S0 : (fine + 1) * S0, :]
        for plane in range(1, 19):
            at = plane * S0
            P0[at : at + S0, :] = post(P0, E0, plane, S0, 1, rows0, plane_mask(plane - 2, 16, ny * 16))
            B0[at : at + S0, :] = B0[at : at + S0, :] + P0[at : at + S0, :]

        for y in range(16):
            at = (y + 2) * S0 + O0
            double(PC, y * 32, pick(P0[at : at + 16, :], index_p))
        coarse_z()
        for d in range(4):
            double(T, d * 32, pick(outer(P0, d), index_p))
        GX[0, :, :] = GX[0, :, :] + T[0:32, :]
        GX[1, :, :] = GX[1, :, :] + T[32:64, :]
        FB[0:32, :] = FA[0:32, :] + T[64:96, :]
        FB[33 * 32 : 34 * 32, :] = FA[33 * 32 : 34 * 32, :] + T[96:128, :]

        def correct(y, _):
            at = pl.ds(pl.multiple_of(y * 32 + 32, 32), 32)
            FB[at, :] = keep32 * (FA[at, :] + PC[pl.ds(pl.multiple_of((y >> 1) * 32, 32), 32), :])
            return 0

        lax.fori_loop(0, 32, correct, 0, unroll=4)

        def last_sweep(y, _):
            def one(k):
                at = pl.multiple_of(k * 32, 32)
                center = FB[pl.ds(at + 32, 32), :]
                around = fine_around(FB, k, center)
                new = keep32 * (G[pl.ds(at, 32), :] + center * (1.0 / 3.0) + around * (1.0 / 9.0))
                FA[pl.ds(at + 32, 32), :] = new
                return new

            both = one(2 * y) + one(2 * y + 1)
            T[pl.ds(pl.multiple_of(y * 32, 32), 32), :] = both
            return 0

        lax.fori_loop(0, 16, last_sweep, 0)
        for y in range(16):
            t = T[pl.ds(y * 32, 16, stride=2), :] + T[pl.ds(y * 32 + 1, 16, stride=2), :]
            means = pick(t + roll(t, -1, 1), index_in) * 0.125
            at = (y + 2) * S0 + O0
            B0[at : at + 16, :] = jnp.where(mask_in16 > 0, means, B0[at : at + 16, :])

    def store_fine(j, _):
        planes = exchange_chunks([FA[pl.ds(pl.multiple_of((4 * j + k + 1) * 32, 32), 32), :] for k in range(4)])
        for s in range(4):
            fout_ref[0, 0, s, :, pl.ds(pl.multiple_of(j * 128, 128), 128)] = planes[s]
        return 0

    lax.fori_loop(0, 8, store_fine, 0)
    for y in range(16):
        at = (y + 2) * S0 + O0
        bout_ref[pl.ds(y, 16, stride=16), :] = B0[at : at + 16, :]
    for dx, dy, copy in pending:
        pl.when(inside(dx, dy))(lambda copy=copy: copy().wait_send())


def solution(mesh):
    nx, ny = mesh.shape["gx"], mesh.shape["gy"]

    def local(fine_rhs, fine_beta, base_rhs, base_beta, slot_site, ghost_list, box_count):
        vmem = pl.BlockSpec(memory_space=pltpu.VMEM)
        smem = pl.BlockSpec(memory_space=pltpu.SMEM)

        def rows(*shape):
            return pltpu.VMEM((*shape, 128), F32)

        fine, base = pl.pallas_call(
            lambda *refs: kernel(nx, ny, *refs),
            out_shape=(
                jax.ShapeDtypeStruct(fine_rhs.shape, F32),
                jax.ShapeDtypeStruct((256, 128), F32),
            ),
            in_specs=[smem] * 3 + [vmem] * 4,
            out_specs=(vmem, vmem),
            scratch_shapes=[
                rows(34 * 32),
                rows(34 * 32),
                rows(32 * 32),
                rows(32 * 32),
                rows(16 * 32),
                rows(16 * 32),
                rows(16 * 32),
                rows(2, 32),
                rows(4 * 32),
                rows(20 * S0),
                rows(20 * S0),
                rows(20 * S0),
                rows(20 * S0),
                rows(20 * S0),
                rows(20 * S0),
                rows(8 * S0),
                rows(18 * S1),
                rows(64),
                rows(18 * S1),
                rows(18 * S1),
                rows(18 * S1),
                rows(8 * S1),
                rows(64),
                rows(64),
                rows(64),
                rows(64),
                rows(16),
                rows(8),
                rows(4, 40),
                rows(8, 40),
                rows(4, 48),
                rows(4, 48),
                rows(2, 4, 32),
                rows(2, 4, 32),
                rows(2, 4, 32),
                rows(2, 4, 8),
                rows(2, 4, 32),
                rows(2, 4, 8),
                rows(2, 4, 40),
                rows(2, 8, 40),
                rows(2, 8),
                rows(2, 7, 8),
                rows(2, 8),
                rows(2, 64),
                pltpu.SemaphoreType.DMA((SEM_COUNT,)),
                pltpu.SemaphoreType.DMA((SEM_COUNT,)),
            ],
            compiler_params=pltpu.CompilerParams(
                collective_id=0, has_side_effects=True, vmem_limit_bytes=48 * 1024 * 1024
            ),
            name="vcycles",
        )(
            slot_site,
            ghost_list,
            box_count,
            fine_rhs,
            fine_beta,
            base_rhs.reshape(256, 128),
            base_beta.reshape(256, 128),
        )
        return fine, base.reshape(16, 16, 128)

    return jax.shard_map(
        local,
        mesh=mesh,
        in_specs=(
            P("gx", "gy", None, None, None),
            P("gx", "gy", None, None, None),
            P("gx", "gy", None),
            P("gx", "gy", None),
            P("gx", "gy", None),
            P("gx", "gy", None, None),
            P("gx", "gy"),
        ),
        out_specs=(P("gx", "gy", None, None, None), P("gx", "gy", None)),
        check_vma=False,
    )
```

```python
import jax
import jax.numpy as jnp
from jax import lax
from jax.experimental import pallas as pl
from jax.experimental.pallas import tpu as pltpu
from jax.sharding import PartitionSpec as P

CYCLES = 2
SWEEPS = 6
MESH = pl.DeviceIdType.MESH
F32 = jnp.float32

S0, O0 = 24, 4
S1, O1 = 24, 8
S2, O2 = 8, 2

DIRS = ((-1, 0), (1, 0), (0, -1), (0, 1), (-1, -1), (-1, 1), (1, -1), (1, 1))
REACH = (-3, -2, -1, 1, 2, 3)
PARTNERS = DIRS + tuple((0, k) for k in (-3, -2, 2, 3)) + tuple((k, 0) for k in (-3, -2, 2, 3))

SEM_COUNT = 8 + 4 + 2 * (4 + 8 + 8 + 6 + 6)


def roll(value, shift, axis):
    return pltpu.roll(value, shift % value.shape[axis], axis)


def tile(value, count):
    return value if count == 1 else jnp.concatenate([value] * count, axis=0)


def pick(value, index):
    parts = [
        jnp.take_along_axis(value[k : k + 8], index, axis=1, mode="promise_in_bounds")
        for k in range(0, value.shape[0], 8)
    ]
    return parts[0] if len(parts) == 1 else jnp.concatenate(parts, axis=0)


def kernel(
    nx,
    ny,
    site_ref,
    link_ref,
    count_ref,
    frhs_hbm,
    fbeta_hbm,
    brhs_hbm,
    bbeta_hbm,
    fout_ref,
    bout_ref,
    frhs_ref,
    fbeta_ref,
    brhs_ref,
    bbeta_ref,
    fetch_sem,
    FA,
    FB,
    G,
    BT,
    PC,
    CGZ,
    T,
    GX,
    CB,
    B0,
    BR,
    C0,
    W0,
    P0,
    E0,
    T0,
    C1,
    W1,
    P1,
    E1,
    U1,
    T1,
    C2,
    W2,
    P2,
    E2,
    T2,
    W3,
    SP,
    RP,
    SA,
    RA,
    SB,
    RB,
    SC,
    SCC,
    RC,
    RCC,
    SD,
    RD,
    SW,
    RW,
    SX,
    RX,
    send_sem,
    recv_sem,
):
    gx = lax.axis_index("gx")
    gy = lax.axis_index("gy")
    counter = [0]
    pending = []

    def inside(dx, dy):
        conds = []
        if dx < 0:
            conds.append(gx >= -dx)
        if dx > 0:
            conds.append(gx < nx - dx)
        if dy < 0:
            conds.append(gy >= -dy)
        if dy > 0:
            conds.append(gy < ny - dy)
        out = conds[0]
        for cond in conds[1:]:
            out = jnp.logical_and(out, cond)
        return out

    def start(messages):
        sent = []
        for dx, dy, source, target in messages:
            k = counter[0]
            counter[0] += 1

            def copy(dx=dx, dy=dy, source=source, target=target, k=k):
                return pltpu.make_async_remote_copy(
                    src_ref=source,
                    dst_ref=target,
                    send_sem=send_sem.at[k],
                    recv_sem=recv_sem.at[k],
                    device_id=(gx + dx, gy + dy),
                    device_id_type=MESH,
                )

            pl.when(inside(dx, dy))(lambda copy=copy: copy().start())
            sent.append((dx, dy, copy))
        pending.extend(sent)
        return sent

    def finish(sent):
        for dx, dy, copy in sent:
            pl.when(inside(-dx, -dy))(lambda copy=copy: copy().wait_recv())

    fetches = [
        pltpu.make_async_copy(fbeta_hbm.at[0, 0], fbeta_ref, fetch_sem.at[0]),
        pltpu.make_async_copy(frhs_hbm.at[0, 0], frhs_ref, fetch_sem.at[1]),
        pltpu.make_async_copy(bbeta_hbm, bbeta_ref, fetch_sem.at[2]),
        pltpu.make_async_copy(brhs_hbm, brhs_ref, fetch_sem.at[3]),
    ]
    for fetch in fetches:
        fetch.start()

    for ref in (RP, RA, RB, RC, RCC, RD, RW, RX):
        ref[...] = jnp.zeros(ref.shape, F32)

    barrier = pltpu.get_barrier_semaphore()
    total = jnp.int32(0)
    for dx, dy in PARTNERS:
        there = inside(dx, dy)

        def greet(dx=dx, dy=dy):
            pl.semaphore_signal(barrier, inc=1, device_id=(gx + dx, gy + dy), device_id_type=MESH)

        pl.when(there)(greet)
        total = total + there.astype(jnp.int32)

    for ref in (B0, BR, C0, W0, P0, E0, C1, P1, E1, U1, FA, FB, GX, CB, SCC):
        ref[...] = jnp.zeros(ref.shape, F32)

    lane = lax.broadcasted_iota(jnp.int32, (8, 128), 1)
    row8 = lax.broadcasted_iota(jnp.int32, (8, 128), 0)
    slot = lane >> 5
    zf = lane & 31
    sites = [site_ref[0, 0, s] for s in range(4)]
    count = count_ref[0, 0]

    def by_slot(values):
        out = jnp.full((8, 128), values[3], jnp.int32)
        for s in (2, 1, 0):
            out = jnp.where(slot == s, values[s], out)
        return out

    site_v = by_slot(sites)
    links = [by_slot([link_ref[0, 0, s, d] for s in range(4)]) for d in range(6)]
    keep8 = jnp.where(slot < count, 1.0, 0.0).astype(F32)
    index_low = jnp.where(zf == 0, jnp.maximum(links[4], 0) * 32 + 31, jnp.maximum(lane - 1, 0))
    index_high = jnp.where(zf == 31, jnp.maximum(links[5], 0) * 32, jnp.minimum(lane + 1, 127))
    mask_low = jnp.where((zf > 0) | (links[4] >= 0), 1.0, 0.0).astype(F32)
    mask_high = jnp.where((zf < 31) | (links[5] >= 0), 1.0, 0.0).astype(F32)
    index_p = site_v * 16 + (zf >> 1)
    index_cz = jnp.where(zf < 16, jnp.maximum(site_v * 16 - 1, 0), jnp.minimum(site_v * 16 + 16, 127))
    mask_cz = jnp.where(
        ((zf == 0) & (links[4] < 0) & (site_v > 0)) | ((zf == 31) & (links[5] < 0) & (site_v < 7)), 1.0, 0.0
    ).astype(F32)
    index_g = [jnp.maximum(links[d], 0) * 32 + zf for d in range(4)]
    mask_g = [jnp.where(links[d] >= 0, 1.0, 0.0).astype(F32) for d in range(4)]
    index_in = jnp.zeros((8, 128), jnp.int32)
    mask_in = jnp.zeros((8, 128), F32)
    for s in range(4):
        held = ((lane >> 4) == sites[s]) & (count > s)
        index_in = jnp.where(held, s * 32 + 2 * (lane & 15), index_in)
        mask_in = jnp.where(held, 1.0, mask_in)
    keep32 = tile(keep8, 4)
    mask_low32 = tile(mask_low, 4)
    mask_high32 = tile(mask_high, 4)
    mask_in16 = tile(mask_in, 2)
    row32 = lax.broadcasted_iota(jnp.int32, (32, 128), 0)
    first32 = jnp.where(row32 == 0, 1.0, 0.0).astype(F32)
    last32 = jnp.where(row32 == 31, 1.0, 0.0).astype(F32)

    lane32 = lax.broadcasted_iota(jnp.int32, (32, 128), 1)
    bit0 = ((lane32 >> 5) & 1) == 0
    bit1 = ((lane32 >> 6) & 1) == 0

    def swap(a, b, bit, shift):
        return jnp.where(bit, a, roll(b, shift, 1)), jnp.where(bit, roll(a, -shift, 1), b)

    def exchange_chunks(parts):
        a, b = swap(parts[0], parts[1], bit0, 32)
        c, d = swap(parts[2], parts[3], bit0, 32)
        a, c = swap(a, c, bit1, 64)
        b, d = swap(b, d, bit1, 64)
        return a, b, c, d

    def load_fine(j, _):
        lanes = pl.ds(pl.multiple_of(j * 128, 128), 128)
        betas = exchange_chunks([fbeta_ref[s, :, lanes] for s in range(4)])
        values = exchange_chunks([frhs_ref[s, :, lanes] for s in range(4)])
        for k in range(4):
            at = pl.multiple_of((4 * j + k) * 32, 32)
            g = values[k] / (9.0 * betas[k])
            BT[pl.ds(at, 32), :] = betas[k]
            G[pl.ds(at, 32), :] = g
            FA[pl.ds(at + 32, 32), :] = g * keep32
        return 0

    fetches[0].wait()
    fetches[1].wait()
    lax.fori_loop(0, 8, load_fine, 0)

    def pack_faces(stage):
        stage[0, 0:32, :] = FA[pl.ds(32, 32, stride=32), :]
        stage[1, 0:32, :] = FA[pl.ds(63, 32, stride=32), :]
        stage[2, 0:32, :] = FA[32:64, :]
        stage[3, 0:32, :] = FA[32 * 32 : 33 * 32, :]

    def send_faces(stage, inbox):
        return start([(*DIRS[d], stage.at[d], inbox.at[d]) for d in range(4)])

    pl.semaphore_wait(barrier, total)
    pack_faces(SB.at[0])
    wait_b = send_faces(SB.at[0], RB.at[0])

    lane8 = lane

    def pair(value, shift):
        wide = lax.broadcasted_iota(jnp.int32, value.shape, 1)
        return value + jnp.where((wide & shift) == 0, roll(value, -shift, 1), roll(value, shift, 1))

    fetches[2].wait()
    fetches[3].wait()
    for y in range(16):
        beta = bbeta_ref[pl.ds(y, 16, stride=16), :]
        c = beta * 0.25
        at = (y + 2) * S0 + O0
        C0[at : at + 16, :] = c
        W0[at : at + 16, :] = 1.0 / (9.0 * c)
        BR[at : at + 16, :] = brhs_ref[pl.ds(y, 16, stride=16), :]

    def restrict0(values, y):
        t = pair(values(2 + 2 * y) + values(3 + 2 * y), 1)
        T0[y * S0 : (y + 1) * S0, :] = t
        return (T0[pl.ds(y * S0 + O0, 8, stride=2), :] + T0[pl.ds(y * S0 + O0 + 1, 8, stride=2), :]) * 0.125

    def restrict1(values, y):
        t = pair(values(1 + 2 * y) + values(2 + 2 * y), 2)
        T1[y * S1 : (y + 1) * S1, :] = t
        return (T1[pl.ds(y * S1 + 4, 8, stride=2), :] + T1[pl.ds(y * S1 + 5, 8, stride=2), :]) * 0.125

    def restrict2(values, y):
        t = pair(values(2 + 2 * y) + values(3 + 2 * y), 4)
        T2[y * S2 : (y + 1) * S2, :] = t
        return (T2[pl.ds(y * S2, 4, stride=2), :] + T2[pl.ds(y * S2 + 1, 4, stride=2), :]) * 0.125

    for y in range(8):
        c = restrict0(lambda p: C0[p * S0 : (p + 1) * S0, :], y) * 0.25
        C1[(y + 5) * S1 + O1 : (y + 5) * S1 + O1 + 8, :] = c
        W1[y * 8 : y * 8 + 8, :] = 1.0 / (9.0 * c)

    def send_level1(ref, stage, inbox):
        for k in range(5):
            stage[0, k * 8 : k * 8 + 8, :] = ref[pl.ds(5 * S1 + O1 + k, 8, stride=S1), :]
            stage[1, k * 8 : k * 8 + 8, :] = ref[pl.ds(5 * S1 + O1 + 3 + k, 8, stride=S1), :]
            stage[2, k * 8 : k * 8 + 8, :] = ref[(5 + k) * S1 + O1 : (5 + k) * S1 + O1 + 8, :]
            stage[3, k * 8 : k * 8 + 8, :] = ref[(8 + k) * S1 + O1 : (8 + k) * S1 + O1 + 8, :]
        source = (0, 1, 2, 3, 2, 3, 2, 3)
        return start([(*DIRS[d], stage.at[source[d]], inbox.at[d]) for d in range(8)])

    def unpack_level1(ref, inbox):
        for k in range(5):
            part = slice(k * 8, k * 8 + 8)
            ref[pl.ds(5 * S1 + 16 + k, 8, stride=S1), :] = inbox[0, part, :]
            ref[pl.ds(5 * S1 + 3 + k, 8, stride=S1), :] = inbox[1, part, :]
            low, high = k * S1, (13 + k) * S1
            ref[high + 8 : high + 16, :] = inbox[2, part, :]
            ref[low + 8 : low + 16, :] = inbox[3, part, :]
            ref[high + 16 : high + 24, :] = inbox[4, part, :]
            ref[low + 16 : low + 24, :] = inbox[5, part, :]
            ref[high : high + 8, :] = inbox[6, part, :]
            ref[low : low + 8, :] = inbox[7, part, :]

    wait_p = send_level1(C1, SP, RP)

    def neighbours(ref, plane, rows, shift):
        c = ref[plane * rows : (plane + 1) * rows, :]
        wide = lax.broadcasted_iota(jnp.int32, (rows, 128), 1)
        total = ref[(plane + 1) * rows : (plane + 2) * rows, :] + ref[(plane - 1) * rows : plane * rows, :]
        total = total + (roll(c, 1, 0) + roll(c, -1, 0))
        low = jnp.where(wide >= shift, roll(c, shift, 1), 0.0)
        high = jnp.where(wide < 128 - shift, roll(c, -shift, 1), 0.0)
        return c, total + (low + high)

    def row_mask(rows, first, extent, count):
        at = lax.broadcasted_iota(jnp.int32, (rows, 128), 0) - first + gx * extent
        return jnp.where((at >= 0) & (at < count), 1.0, 0.0).astype(F32)

    def plane_mask(y, extent, count):
        at = y + gy * extent
        return jnp.where((at >= 0) & (at < count), 1.0, 0.0).astype(F32)

    rows0 = row_mask(S0, O0, 16, nx * 16)
    rows1 = row_mask(S1, O1, 8, nx * 8)
    rows2 = row_mask(S2, O2, 4, nx * 4)

    def post(pre, field, plane, rows, shift, mask, scale):
        c, around = neighbours(field, plane, rows, shift)
        return pre[plane * rows : (plane + 1) * rows, :] + (mask * scale) * (c * (1.0 / 3.0) + around * (1.0 / 9.0))

    def fine_around(field, y, center, edges=True):
        at = pl.multiple_of(y * 32, 32)
        total = field[pl.ds(at, 32), :] + field[pl.ds(at + 64, 32), :]
        low = jnp.broadcast_to(GX[0, pl.ds(y, 1), :], (32, 128)) if edges else 0.0
        high = jnp.broadcast_to(GX[1, pl.ds(y, 1), :], (32, 128)) if edges else 0.0
        total = total + jnp.where(first32 > 0, low, roll(center, 1, 0)) + jnp.where(last32 > 0, high, roll(center, -1, 0))
        total = total + (pick(center, index_low) * mask_low32 + pick(center, index_high) * mask_high32)
        return total + CGZ[pl.ds(pl.multiple_of((y >> 1) * 32, 32), 32), :]

    def restrict_fine(values, y):
        at = pl.multiple_of(y * 32, 32)
        T[pl.ds(at, 32), :] = values
        t = T[pl.ds(at, 16, stride=2), :] + T[pl.ds(at + 1, 16, stride=2), :]
        return pick(t + roll(t, -1, 1), index_in) * 0.125

    def double(ref, at, value):
        ref[pl.ds(at, value.shape[0], stride=2), :] = value
        ref[pl.ds(at + 1, value.shape[0], stride=2), :] = value

    def set_ghosts(inbox):
        GX[0, :, :] = pick(inbox[1, 0:32, :], index_g[0]) * tile(mask_g[0], 4) + CB[0:32, :]
        GX[1, :, :] = pick(inbox[0, 0:32, :], index_g[1]) * tile(mask_g[1], 4) + CB[32:64, :]
        FA[0:32, :] = pick(inbox[3, 0:32, :], index_g[2]) * tile(mask_g[2], 4) + CB[64:96, :]
        FA[33 * 32 : 34 * 32, :] = pick(inbox[2, 0:32, :], index_g[3]) * tile(mask_g[3], 4) + CB[96:128, :]

    def clear_y_ghosts():
        FA[0:32, :] = jnp.zeros((32, 128), F32)
        FA[33 * 32 : 34 * 32, :] = jnp.zeros((32, 128), F32)

    def outer(ref, d):
        if d == 0:
            return ref[pl.ds(2 * S0 + O0 - 1, 16, stride=S0), :]
        if d == 1:
            return ref[pl.ds(2 * S0 + O0 + 16, 16, stride=S0), :]
        plane = 1 if d == 2 else 18
        return ref[plane * S0 + O0 : plane * S0 + O0 + 16, :]

    def coarse_z():
        for y in range(16):
            at = (y + 2) * S0 + O0
            double(CGZ, y * 32, pick(B0[at : at + 16, :], index_cz) * tile(mask_cz, 2))

    for cycle in range(CYCLES):
        if cycle == 0:
            CGZ[...] = jnp.zeros(CGZ.shape, F32)
        else:
            pack_faces(SA)
            SA[0, 32:48, :] = B0[pl.ds(2 * S0 + O0, 16, stride=S0), :]
            SA[1, 32:48, :] = B0[pl.ds(2 * S0 + O0 + 15, 16, stride=S0), :]
            SA[2, 32:48, :] = B0[2 * S0 + O0 : 2 * S0 + O0 + 16, :]
            SA[3, 32:48, :] = B0[17 * S0 + O0 : 17 * S0 + O0 + 16, :]
            wait_a = send_faces(SA, RA)
            coarse_z()
            clear_y_ghosts()

            def first_sweep(y, _):
                at = pl.multiple_of(y * 32, 32)
                center = FA[pl.ds(at + 32, 32), :]
                around = fine_around(FA, y, center, False)
                FB[pl.ds(at + 32, 32), :] = keep32 * (
                    G[pl.ds(at, 32), :] + center * (1.0 / 3.0) + around * (1.0 / 9.0)
                )
                return 0

            lax.fori_loop(0, 32, first_sweep, 0, unroll=2)
            finish(wait_a)
            B0[pl.ds(2 * S0 + O0 + 16, 16, stride=S0), :] = RA[0, 32:48, :]
            B0[pl.ds(2 * S0 + O0 - 1, 16, stride=S0), :] = RA[1, 32:48, :]
            B0[18 * S0 + O0 : 18 * S0 + O0 + 16, :] = RA[2, 32:48, :]
            B0[1 * S0 + O0 : 1 * S0 + O0 + 16, :] = RA[3, 32:48, :]
            for d in range(4):
                double(CB, d * 32, pick(outer(B0, d), index_p) * tile(1.0 - mask_g[d], 2))
            set_ghosts(RA)

            ninth = keep32 * (1.0 / 9.0)
            FB[32:64, :] = FB[32:64, :] + ninth * FA[0:32, :]
            FB[32 * 32 : 33 * 32, :] = FB[32 * 32 : 33 * 32, :] + ninth * FA[33 * 32 : 34 * 32, :]
            for d, first in enumerate((32, 63)):
                face = pl.ds(first, 32, stride=32)
                FB[face, :] = FB[face, :] + ninth * GX[d, :, :]
            FA, FB = FB, FA
            pack_faces(SB.at[cycle])
            wait_b = send_faces(SB.at[cycle], RB.at[cycle])

        if cycle == 0:
            for y in range(16):
                at = (y + 2) * S0
                P0[at : at + S0, :] = BR[at : at + S0, :]
        else:
            for y in range(16):
                at = (y + 2) * S0
                c, around = neighbours(B0, y + 2, S0, 1)
                P0[at : at + S0, :] = BR[at : at + S0, :] - C0[at : at + S0, :] * (6.0 * c - around)

        clear_y_ghosts()

        def residual(y, _):
            def one(k):
                at = pl.multiple_of(k * 32, 32)
                center = FA[pl.ds(at + 32, 32), :]
                around = fine_around(FA, k, center, False)
                return BT[pl.ds(at, 32), :] * (9.0 * G[pl.ds(at, 32), :] - 6.0 * center + around)

            both = one(2 * y) + one(2 * y + 1)
            T[pl.ds(pl.multiple_of(y * 32, 32), 32), :] = both
            return 0

        lax.fori_loop(0, 16, residual, 0)
        finish(wait_b)
        set_ghosts(RB.at[cycle])
        T[0:32, :] = T[0:32, :] + BT[0:32, :] * FA[0:32, :]
        T[480:512, :] = T[480:512, :] + BT[31 * 32 : 32 * 32, :] * FA[33 * 32 : 34 * 32, :]
        for d, first in enumerate((0, 31)):
            face = pl.ds(first, 16, stride=32)
            T[face, :] = (
                T[face, :]
                + BT[pl.ds(first, 16, stride=64), :] * GX[d, pl.ds(0, 16, stride=2), :]
                + BT[pl.ds(first + 32, 16, stride=64), :] * GX[d, pl.ds(1, 16, stride=2), :]
            )
        for y in range(16):
            t = T[pl.ds(y * 32, 16, stride=2), :] + T[pl.ds(y * 32 + 1, 16, stride=2), :]
            means = pick(t + roll(t, -1, 1), index_in) * 0.125
            at = (y + 2) * S0 + O0
            P0[at : at + 16, :] = jnp.where(mask_in16 > 0, means, P0[at : at + 16, :]) * W0[at : at + 16, :]

        stage, corner = SC.at[cycle], SCC.at[cycle]
        for k in range(2):
            part = slice(k * 16, k * 16 + 16)
            stage[0, part, :] = P0[pl.ds(2 * S0 + O0 + k, 16, stride=S0), :]
            stage[1, part, :] = P0[pl.ds(2 * S0 + O0 + 14 + k, 16, stride=S0), :]
            stage[2, part, :] = P0[(2 + k) * S0 + O0 : (2 + k) * S0 + O0 + 16, :]
            stage[3, part, :] = P0[(16 + k) * S0 + O0 : (16 + k) * S0 + O0 + 16, :]
            for d in range(4):
                dx, dy = DIRS[4 + d]
                at = ((2 if dy < 0 else 16) + k) * S0 + O0 + (0 if dx < 0 else 14)
                corner[d, 2 * k : 2 * k + 2, :] = P0[at : at + 2, :]
        inbox, corners = RC.at[cycle], RCC.at[cycle]
        wait_c = start([(*DIRS[d], stage.at[d], inbox.at[d]) for d in range(4)])
        wait_cc = start([(*DIRS[4 + d], corner.at[d], corners.at[d]) for d in range(4)])
        finish(wait_c)
        for k in range(2):
            part = slice(k * 16, k * 16 + 16)
            P0[pl.ds(2 * S0 + O0 + 16 + k, 16, stride=S0), :] = inbox[0, part, :]
            P0[pl.ds(2 * S0 + O0 - 2 + k, 16, stride=S0), :] = inbox[1, part, :]
            P0[(18 + k) * S0 + O0 : (18 + k) * S0 + O0 + 16, :] = inbox[2, part, :]
            P0[k * S0 + O0 : k * S0 + O0 + 16, :] = inbox[3, part, :]

        def left0(plane):
            c, around = neighbours(P0, plane, S0, 1)
            return C0[plane * S0 : (plane + 1) * S0, :] * (3.0 * c + around)

        for y in range(8):
            at = (y + 5) * S1 + O1
            P1[at : at + 8, :] = restrict0(left0, y) * W1[y * 8 : y * 8 + 8, :]
        wait_d = send_level1(P1, SD.at[cycle], RD.at[cycle])
        if cycle == 0:
            finish(wait_p)
            unpack_level1(C1, RP)
            for y in range(8):
                c = restrict1(lambda p: C1[p * S1 : (p + 1) * S1, :], y) * 0.25
                C2[y * 8 : y * 8 + 8, :] = c
                W2[y * 8 : y * 8 + 8, :] = jnp.where(c > 0, 1.0 / (9.0 * jnp.where(c > 0, c, 1.0)), 0.0)
            for y in range(2):
                c = restrict2(lambda p: C2[p * S2 : (p + 1) * S2, :], y) * 0.25
                W3[y * 4 : y * 4 + 4, :] = jnp.where(c > 0, 1.0 / (9.0 * jnp.where(c > 0, c, 1.0)), 0.0)
        finish(wait_cc)
        for k in range(2):
            for d in range(4):
                dx, dy = DIRS[4 + d]
                at = ((18 if dy < 0 else 0) + k) * S0 + (O0 + 16 if dx < 0 else O0 - 2)
                P0[at : at + 2, :] = corners[d, 2 * k : 2 * k + 2, :]
        finish(wait_d)
        unpack_level1(P1, RD.at[cycle])

        def left1(plane):
            c, around = neighbours(P1, plane, S1, 2)
            return C1[plane * S1 : (plane + 1) * S1, :] * (3.0 * c + around)

        for y in range(8):
            P2[y * 8 : y * 8 + 8, :] = restrict1(left1, y) * W2[y * 8 : y * 8 + 8, :]

        def left2(plane):
            c, around = neighbours(P2, plane, S2, 4)
            return C2[plane * S2 : (plane + 1) * S2, :] * (3.0 * c + around)

        mine = jnp.concatenate([restrict2(left2, y) for y in range(2)], axis=0) * W3[...]
        strip = SW.at[cycle]
        strip[...] = pick(mine, (lane8 & 15) * 8)
        wait_w = start([(0, k, strip, RW.at[cycle, 3 - k]) for k in REACH])
        finish(wait_w)
        joined = jnp.where((lane8 >> 4) == 3, strip[...], 0.0)
        for k in REACH:
            joined = jnp.where((lane8 >> 4) == 3 + k, RW[cycle, 3 + k, :, :], joined)
        SX[cycle, :, :] = joined
        wait_x = start([(k, 0, SX.at[cycle], RX.at[cycle, pl.ds((3 - k) * 8, 8)]) for k in REACH])
        RX[cycle, 24:32, :] = joined
        finish(wait_x)

        first = [[RX[cycle, pl.ds(y * 4 + 1 + x, 8, stride=8), :] for x in range(2)] for y in range(2)]
        col_x = gx + row8 - 3
        col_y = gy + (lane8 >> 4) - 3
        there = (col_x >= 0) & (col_x < nx) & (row8 < 7) & (col_y >= 0) & (col_y < ny) & (lane8 < 112)
        mask3 = jnp.where(there, 1.0, 0.0).astype(F32)
        e = first
        for sweep in range(SWEEPS - 1):
            new = [[None, None], [None, None]]
            for y in range(2):
                for x in range(2):
                    c, ex, ey = e[y][x], e[y][1 - x], e[1 - y][x]
                    around = ex + roll(ex, 1 if x == 0 else -1, 0) + ey + roll(ey, 16 if y == 0 else -16, 1)
                    around = around + jnp.where((lane8 & 15) > 0, roll(c, 1, 1), 0.0)
                    around = around + jnp.where((lane8 & 15) < 15, roll(c, -1, 1), 0.0)
                    new[y][x] = first[y][x] + mask3 * (c * (1.0 / 3.0) + around * (1.0 / 9.0))
            e = new

        from_one = jnp.where(row8 < 2, 2, 3)
        from_zero = jnp.where(row8 < 4, 3, 4)
        for k, (column, y) in enumerate(((2, 1), (3, 0), (3, 1), (4, 0))):
            lanes = column * 16 + (lane8 >> 3)
            zero, one = pick(e[y][0], lanes), pick(e[y][1], lanes)
            zero = jnp.take_along_axis(zero, from_zero, axis=0, mode="promise_in_bounds")
            one = jnp.take_along_axis(one, from_one, axis=0, mode="promise_in_bounds")
            up = jnp.where((row8 & 2) == 0, one, zero)
            for plane in (2 * k, 2 * k + 1):
                E2[plane * 8 : plane * 8 + 8, :] = P2[plane * 8 : plane * 8 + 8, :] + up
        for plane in range(1, 7):
            up = post(P2, E2, plane, S2, 4, rows2, plane_mask(plane - 2, 4, ny * 4))
            at = plane * S1
            double(U1, at + 4, up)
            for fine in (2 * plane + 1, 2 * plane + 2):
                E1[fine * S1 : (fine + 1) * S1, :] = P1[fine * S1 : (fine + 1) * S1, :] + U1[at : at + S1, :]
        for plane in range(4, 14):
            at = plane * S1
            U1[at : at + S1, :] = post(P1, E1, plane, S1, 2, rows1, plane_mask(plane - 5, 8, ny * 8))
            value = U1[at + 7 : at + 17, :]
            fine = 2 * (plane - 4)
            double(E0, fine * S0 + 2, value)
            up = E0[fine * S0 : (fine + 1) * S0, :]
            E0[(fine + 1) * S0 : (fine + 2) * S0, :] = up + P0[(fine + 1) * S0 : (fine + 2) * S0, :]
            E0[fine * S0 : (fine + 1) * S0, :] = up + P0[fine * S0 : (fine + 1) * S0, :]
        for plane in range(1, 19):
            at = plane * S0
            P0[at : at + S0, :] = post(P0, E0, plane, S0, 1, rows0, plane_mask(plane - 2, 16, ny * 16))
            B0[at : at + S0, :] = B0[at : at + S0, :] + P0[at : at + S0, :]

        for y in range(16):
            at = (y + 2) * S0 + O0
            double(PC, y * 32, pick(P0[at : at + 16, :], index_p))
        coarse_z()
        for d in range(4):
            double(T, d * 32, pick(outer(P0, d), index_p))
        GX[0, :, :] = GX[0, :, :] + T[0:32, :]
        GX[1, :, :] = GX[1, :, :] + T[32:64, :]
        FB[0:32, :] = FA[0:32, :] + T[64:96, :]
        FB[33 * 32 : 34 * 32, :] = FA[33 * 32 : 34 * 32, :] + T[96:128, :]

        def correct(y, _):
            at = pl.ds(pl.multiple_of(y * 32 + 32, 32), 32)
            FB[at, :] = keep32 * (FA[at, :] + PC[pl.ds(pl.multiple_of((y >> 1) * 32, 32), 32), :])
            return 0

        lax.fori_loop(0, 32, correct, 0, unroll=4)

        def last_sweep(y, _):
            def one(k):
                at = pl.multiple_of(k * 32, 32)
                center = FB[pl.ds(at + 32, 32), :]
                around = fine_around(FB, k, center)
                new = keep32 * (G[pl.ds(at, 32), :] + center * (1.0 / 3.0) + around * (1.0 / 9.0))
                FA[pl.ds(at + 32, 32), :] = new
                return new

            both = one(2 * y) + one(2 * y + 1)
            T[pl.ds(pl.multiple_of(y * 32, 32), 32), :] = both
            return 0

        lax.fori_loop(0, 16, last_sweep, 0)
        for y in range(16):
            t = T[pl.ds(y * 32, 16, stride=2), :] + T[pl.ds(y * 32 + 1, 16, stride=2), :]
            means = pick(t + roll(t, -1, 1), index_in) * 0.125
            at = (y + 2) * S0 + O0
            B0[at : at + 16, :] = jnp.where(mask_in16 > 0, means, B0[at : at + 16, :])

    def store_fine(j, _):
        planes = exchange_chunks([FA[pl.ds(pl.multiple_of((4 * j + k + 1) * 32, 32), 32), :] for k in range(4)])
        for s in range(4):
            fout_ref[0, 0, s, :, pl.ds(pl.multiple_of(j * 128, 128), 128)] = planes[s]
        return 0

    lax.fori_loop(0, 8, store_fine, 0)
    for y in range(16):
        at = (y + 2) * S0 + O0
        bout_ref[pl.ds(y, 16, stride=16), :] = B0[at : at + 16, :]
    for dx, dy, copy in pending:
        pl.when(inside(dx, dy))(lambda copy=copy: copy().wait_send())


def solution(mesh):
    nx, ny = mesh.shape["gx"], mesh.shape["gy"]

    def local(fine_rhs, fine_beta, base_rhs, base_beta, slot_site, ghost_list, box_count):
        vmem = pl.BlockSpec(memory_space=pltpu.VMEM)
        smem = pl.BlockSpec(memory_space=pltpu.SMEM)

        def rows(*shape):
            return pltpu.VMEM((*shape, 128), F32)

        fine, base = pl.pallas_call(
            lambda *refs: kernel(nx, ny, *refs),
            out_shape=(
                jax.ShapeDtypeStruct(fine_rhs.shape, F32),
                jax.ShapeDtypeStruct((256, 128), F32),
            ),
            in_specs=[smem] * 3 + [pl.BlockSpec(memory_space=pltpu.HBM)] * 4,
            out_specs=(vmem, vmem),
            scratch_shapes=[
                pltpu.VMEM(fine_rhs.shape[2:], F32),
                pltpu.VMEM(fine_rhs.shape[2:], F32),
                rows(256),
                rows(256),
                pltpu.SemaphoreType.DMA((4,)),
                rows(34 * 32),
                rows(34 * 32),
                rows(32 * 32),
                rows(32 * 32),
                rows(16 * 32),
                rows(16 * 32),
                rows(16 * 32),
                rows(2, 32),
                rows(4 * 32),
                rows(20 * S0),
                rows(20 * S0),
                rows(20 * S0),
                rows(20 * S0),
                rows(20 * S0),
                rows(20 * S0),
                rows(8 * S0),
                rows(18 * S1),
                rows(64),
                rows(18 * S1),
                rows(18 * S1),
                rows(18 * S1),
                rows(8 * S1),
                rows(64),
                rows(64),
                rows(64),
                rows(64),
                rows(16),
                rows(8),
                rows(4, 40),
                rows(8, 40),
                rows(4, 48),
                rows(4, 48),
                rows(2, 4, 32),
                rows(2, 4, 32),
                rows(2, 4, 32),
                rows(2, 4, 8),
                rows(2, 4, 32),
                rows(2, 4, 8),
                rows(2, 4, 40),
                rows(2, 8, 40),
                rows(2, 8),
                rows(2, 7, 8),
                rows(2, 8),
                rows(2, 64),
                pltpu.SemaphoreType.DMA((SEM_COUNT,)),
                pltpu.SemaphoreType.DMA((SEM_COUNT,)),
            ],
            compiler_params=pltpu.CompilerParams(
                collective_id=0, has_side_effects=True, vmem_limit_bytes=48_000_000
            ),
            name="vcycles",
        )(
            pltpu.with_memory_space_constraint(slot_site, pltpu.HBM),
            pltpu.with_memory_space_constraint(ghost_list, pltpu.HBM),
            box_count,
            pltpu.with_memory_space_constraint(fine_rhs, pltpu.HBM),
            pltpu.with_memory_space_constraint(fine_beta, pltpu.HBM),
            pltpu.with_memory_space_constraint(base_rhs.reshape(256, 128), pltpu.HBM),
            pltpu.with_memory_space_constraint(base_beta.reshape(256, 128), pltpu.HBM),
        )
        return fine, base.reshape(16, 16, 128)

    return jax.shard_map(
        local,
        mesh=mesh,
        in_specs=(
            P("gx", "gy", None, None, None),
            P("gx", "gy", None, None, None),
            P("gx", "gy", None),
            P("gx", "gy", None),
            P("gx", "gy", None),
            P("gx", "gy", None, None),
            P("gx", "gy"),
        ),
        out_specs=(P("gx", "gy", None, None, None), P("gx", "gy", None)),
        check_vma=False,
    )
```

```python
import jax
import jax.numpy as jnp
from jax import lax
from jax.experimental import pallas as pl
from jax.experimental.pallas import tpu as pltpu
from jax.sharding import PartitionSpec as P

CYCLES = 2
SWEEPS = 6
MESH = pl.DeviceIdType.MESH
F32 = jnp.float32

S0, O0 = 24, 4
S1, O1 = 24, 8
S2, O2 = 8, 2

DIRS = ((-1, 0), (1, 0), (0, -1), (0, 1), (-1, -1), (-1, 1), (1, -1), (1, 1))
REACH = (-3, -2, -1, 1, 2, 3)
PARTNERS = DIRS + tuple((0, k) for k in (-3, -2, 2, 3)) + tuple((k, 0) for k in (-3, -2, 2, 3))

SEM_COUNT = 8 + 4 + 2 * (4 + 8 + 8 + 6 + 6)


def roll(value, shift, axis):
    return pltpu.roll(value, shift % value.shape[axis], axis)


def tile(value, count):
    return value if count == 1 else jnp.concatenate([value] * count, axis=0)


def pick(value, index):
    parts = [
        jnp.take_along_axis(value[k : k + 8], index, axis=1, mode="promise_in_bounds")
        for k in range(0, value.shape[0], 8)
    ]
    return parts[0] if len(parts) == 1 else jnp.concatenate(parts, axis=0)


def kernel(
    nx,
    ny,
    site_ref,
    link_ref,
    count_ref,
    frhs_hbm,
    fbeta_hbm,
    brhs_hbm,
    bbeta_hbm,
    fout_ref,
    bout_ref,
    frhs_ref,
    fbeta_ref,
    brhs_ref,
    bbeta_ref,
    fetch_sem,
    FA,
    FB,
    G,
    BT,
    PC,
    CGZ,
    T,
    GX,
    CB,
    B0,
    BR,
    C0,
    W0,
    P0,
    E0,
    T0,
    C1,
    W1,
    P1,
    E1,
    U1,
    T1,
    C2,
    W2,
    P2,
    E2,
    T2,
    W3,
    SP,
    RP,
    SA,
    RA,
    SB,
    RB,
    SC,
    SCC,
    RC,
    RCC,
    SD,
    RD,
    SW,
    RW,
    SX,
    RX,
    send_sem,
    recv_sem,
):
    gx = lax.axis_index("gx")
    gy = lax.axis_index("gy")
    counter = [0]
    pending = []

    def inside(dx, dy):
        conds = []
        if dx < 0:
            conds.append(gx >= -dx)
        if dx > 0:
            conds.append(gx < nx - dx)
        if dy < 0:
            conds.append(gy >= -dy)
        if dy > 0:
            conds.append(gy < ny - dy)
        out = conds[0]
        for cond in conds[1:]:
            out = jnp.logical_and(out, cond)
        return out

    def start(messages):
        sent = []
        for dx, dy, source, target in messages:
            k = counter[0]
            counter[0] += 1

            def copy(dx=dx, dy=dy, source=source, target=target, k=k):
                return pltpu.make_async_remote_copy(
                    src_ref=source,
                    dst_ref=target,
                    send_sem=send_sem.at[k],
                    recv_sem=recv_sem.at[k],
                    device_id=(gx + dx, gy + dy),
                    device_id_type=MESH,
                )

            pl.when(inside(dx, dy))(lambda copy=copy: copy().start())
            sent.append((dx, dy, copy))
        pending.extend(sent)
        return sent

    def finish(sent):
        for dx, dy, copy in sent:
            pl.when(inside(-dx, -dy))(lambda copy=copy: copy().wait_recv())

    fetches = [
        pltpu.make_async_copy(fbeta_hbm.at[0, 0], fbeta_ref, fetch_sem.at[0]),
        pltpu.make_async_copy(frhs_hbm.at[0, 0], frhs_ref, fetch_sem.at[1]),
        pltpu.make_async_copy(bbeta_hbm, bbeta_ref, fetch_sem.at[2]),
        pltpu.make_async_copy(brhs_hbm, brhs_ref, fetch_sem.at[3]),
    ]
    for fetch in fetches:
        fetch.start()

    for ref in (RP, RA, RB, RC, RCC, RD, RW, RX):
        ref[...] = jnp.zeros(ref.shape, F32)

    barrier = pltpu.get_barrier_semaphore()
    total = jnp.int32(0)
    for dx, dy in PARTNERS:
        there = inside(dx, dy)

        def greet(dx=dx, dy=dy):
            pl.semaphore_signal(barrier, inc=1, device_id=(gx + dx, gy + dy), device_id_type=MESH)

        pl.when(there)(greet)
        total = total + there.astype(jnp.int32)

    for ref in (B0, BR, C0, W0, P0, E0, C1, P1, E1, U1, FA, FB, GX, CB, SCC):
        ref[...] = jnp.zeros(ref.shape, F32)

    lane = lax.broadcasted_iota(jnp.int32, (8, 128), 1)
    row8 = lax.broadcasted_iota(jnp.int32, (8, 128), 0)
    slot = lane >> 5
    zf = lane & 31
    sites = [site_ref[0, 0, s] for s in range(4)]
    count = count_ref[0, 0]

    def by_slot(values):
        out = jnp.full((8, 128), values[3], jnp.int32)
        for s in (2, 1, 0):
            out = jnp.where(slot == s, values[s], out)
        return out

    site_v = by_slot(sites)
    links = [by_slot([link_ref[0, 0, s, d] for s in range(4)]) for d in range(6)]
    keep8 = jnp.where(slot < count, 1.0, 0.0).astype(F32)
    index_low = jnp.where(zf == 0, jnp.maximum(links[4], 0) * 32 + 31, jnp.maximum(lane - 1, 0))
    index_high = jnp.where(zf == 31, jnp.maximum(links[5], 0) * 32, jnp.minimum(lane + 1, 127))
    mask_low = jnp.where((zf > 0) | (links[4] >= 0), 1.0, 0.0).astype(F32)
    mask_high = jnp.where((zf < 31) | (links[5] >= 0), 1.0, 0.0).astype(F32)
    index_p = site_v * 16 + (zf >> 1)
    index_cz = jnp.where(zf < 16, jnp.maximum(site_v * 16 - 1, 0), jnp.minimum(site_v * 16 + 16, 127))
    mask_cz = jnp.where(
        ((zf == 0) & (links[4] < 0) & (site_v > 0)) | ((zf == 31) & (links[5] < 0) & (site_v < 7)), 1.0, 0.0
    ).astype(F32)
    index_g = [jnp.maximum(links[d], 0) * 32 + zf for d in range(4)]
    mask_g = [jnp.where(links[d] >= 0, 1.0, 0.0).astype(F32) for d in range(4)]
    index_in = jnp.zeros((8, 128), jnp.int32)
    mask_in = jnp.zeros((8, 128), F32)
    for s in range(4):
        held = ((lane >> 4) == sites[s]) & (count > s)
        index_in = jnp.where(held, s * 32 + 2 * (lane & 15), index_in)
        mask_in = jnp.where(held, 1.0, mask_in)
    keep32 = tile(keep8, 4)
    mask_low32 = tile(mask_low, 4)
    mask_high32 = tile(mask_high, 4)
    mask_in16 = tile(mask_in, 2)
    row32 = lax.broadcasted_iota(jnp.int32, (32, 128), 0)
    first32 = jnp.where(row32 == 0, 1.0, 0.0).astype(F32)
    last32 = jnp.where(row32 == 31, 1.0, 0.0).astype(F32)

    lane32 = lax.broadcasted_iota(jnp.int32, (32, 128), 1)
    bit0 = ((lane32 >> 5) & 1) == 0
    bit1 = ((lane32 >> 6) & 1) == 0

    def swap(a, b, bit, shift):
        return jnp.where(bit, a, roll(b, shift, 1)), jnp.where(bit, roll(a, -shift, 1), b)

    def exchange_chunks(parts):
        a, b = swap(parts[0], parts[1], bit0, 32)
        c, d = swap(parts[2], parts[3], bit0, 32)
        a, c = swap(a, c, bit1, 64)
        b, d = swap(b, d, bit1, 64)
        return a, b, c, d

    def load_fine(j, _):
        lanes = pl.ds(pl.multiple_of(j * 128, 128), 128)
        betas = exchange_chunks([fbeta_ref[s, :, lanes] for s in range(4)])
        values = exchange_chunks([frhs_ref[s, :, lanes] for s in range(4)])
        for k in range(4):
            at = pl.multiple_of((4 * j + k) * 32, 32)
            g = values[k] / (9.0 * betas[k])
            BT[pl.ds(at, 32), :] = betas[k]
            G[pl.ds(at, 32), :] = g
            FA[pl.ds(at + 32, 32), :] = g * keep32
        return 0

    fetches[0].wait()
    fetches[1].wait()
    lax.fori_loop(0, 8, load_fine, 0, unroll=2)

    def pack_faces(stage):
        stage[0, 0:32, :] = FA[pl.ds(32, 32, stride=32), :]
        stage[1, 0:32, :] = FA[pl.ds(63, 32, stride=32), :]
        stage[2, 0:32, :] = FA[32:64, :]
        stage[3, 0:32, :] = FA[32 * 32 : 33 * 32, :]

    def send_faces(stage, inbox):
        return start([(*DIRS[d], stage.at[d], inbox.at[d]) for d in range(4)])

    pl.semaphore_wait(barrier, total)
    pack_faces(SB.at[0])
    wait_b = send_faces(SB.at[0], RB.at[0])

    lane8 = lane

    def pair(value, shift):
        wide = lax.broadcasted_iota(jnp.int32, value.shape, 1)
        return value + jnp.where((wide & shift) == 0, roll(value, -shift, 1), roll(value, shift, 1))

    fetches[2].wait()
    fetches[3].wait()
    for y in range(16):
        beta = bbeta_ref[pl.ds(y, 16, stride=16), :]
        c = beta * 0.25
        at = (y + 2) * S0 + O0
        C0[at : at + 16, :] = c
        W0[at : at + 16, :] = 1.0 / (9.0 * c)
        BR[at : at + 16, :] = brhs_ref[pl.ds(y, 16, stride=16), :]

    def restrict0(values, y):
        t = pair(values(2 + 2 * y) + values(3 + 2 * y), 1)
        T0[y * S0 : (y + 1) * S0, :] = t
        return (T0[pl.ds(y * S0 + O0, 8, stride=2), :] + T0[pl.ds(y * S0 + O0 + 1, 8, stride=2), :]) * 0.125

    def restrict1(values, y):
        t = pair(values(1 + 2 * y) + values(2 + 2 * y), 2)
        T1[y * S1 : (y + 1) * S1, :] = t
        return (T1[pl.ds(y * S1 + 4, 8, stride=2), :] + T1[pl.ds(y * S1 + 5, 8, stride=2), :]) * 0.125

    def restrict2(values, y):
        t = pair(values(2 + 2 * y) + values(3 + 2 * y), 4)
        T2[y * S2 : (y + 1) * S2, :] = t
        return (T2[pl.ds(y * S2, 4, stride=2), :] + T2[pl.ds(y * S2 + 1, 4, stride=2), :]) * 0.125

    for y in range(8):
        c = restrict0(lambda p: C0[p * S0 : (p + 1) * S0, :], y) * 0.25
        C1[(y + 5) * S1 + O1 : (y + 5) * S1 + O1 + 8, :] = c
        W1[y * 8 : y * 8 + 8, :] = 1.0 / (9.0 * c)

    odd = (lane & 1) == 1

    def send_level1(ref, stage, inbox):
        def fill(d, tiles):
            stage[d, 0:8, :] = jnp.where(odd, tiles[1], tiles[0])
            stage[d, 8:16, :] = jnp.where(odd, tiles[3], tiles[2])
            stage[d, 16:24, :] = tiles[4]

        fill(0, [ref[pl.ds(5 * S1 + O1 + k, 8, stride=S1), :] for k in range(5)])
        fill(1, [ref[pl.ds(5 * S1 + O1 + 3 + k, 8, stride=S1), :] for k in range(5)])
        fill(2, [ref[(5 + k) * S1 + O1 : (5 + k) * S1 + O1 + 8, :] for k in range(5)])
        fill(3, [ref[(8 + k) * S1 + O1 : (8 + k) * S1 + O1 + 8, :] for k in range(5)])
        source = (0, 1, 2, 3, 2, 3, 2, 3)
        return start([(*DIRS[d], stage.at[source[d]], inbox.at[d]) for d in range(8)])

    def unpack_level1(ref, inbox):
        def tiles(d):
            out = []
            for k in range(2):
                both = inbox[d, k * 8 : k * 8 + 8, :]
                out.append(jnp.where(odd, roll(both, 1, 1), both))
                out.append(jnp.where(odd, both, roll(both, -1, 1)))
            return out + [inbox[d, 16:24, :]]

        got = [tiles(d) for d in range(8)]
        for k in range(5):
            ref[pl.ds(5 * S1 + 16 + k, 8, stride=S1), :] = got[0][k]
            ref[pl.ds(5 * S1 + 3 + k, 8, stride=S1), :] = got[1][k]
            low, high = k * S1, (13 + k) * S1
            ref[high + 8 : high + 16, :] = got[2][k]
            ref[low + 8 : low + 16, :] = got[3][k]
            ref[high + 16 : high + 24, :] = got[4][k]
            ref[low + 16 : low + 24, :] = got[5][k]
            ref[high : high + 8, :] = got[6][k]
            ref[low : low + 8, :] = got[7][k]

    wait_p = send_level1(C1, SP, RP)

    def neighbours(ref, plane, rows, shift):
        c = ref[plane * rows : (plane + 1) * rows, :]
        wide = lax.broadcasted_iota(jnp.int32, (rows, 128), 1)
        total = ref[(plane + 1) * rows : (plane + 2) * rows, :] + ref[(plane - 1) * rows : plane * rows, :]
        total = total + (roll(c, 1, 0) + roll(c, -1, 0))
        low = jnp.where(wide >= shift, roll(c, shift, 1), 0.0)
        high = jnp.where(wide < 128 - shift, roll(c, -shift, 1), 0.0)
        return c, total + (low + high)

    def row_mask(rows, first, extent, count):
        at = lax.broadcasted_iota(jnp.int32, (rows, 128), 0) - first + gx * extent
        return jnp.where((at >= 0) & (at < count), 1.0, 0.0).astype(F32)

    def plane_mask(y, extent, count):
        at = y + gy * extent
        return jnp.where((at >= 0) & (at < count), 1.0, 0.0).astype(F32)

    rows0 = row_mask(S0, O0, 16, nx * 16)
    rows1 = row_mask(S1, O1, 8, nx * 8)
    rows2 = row_mask(S2, O2, 4, nx * 4)

    def post(pre, field, plane, rows, shift, mask, scale):
        c, around = neighbours(field, plane, rows, shift)
        return pre[plane * rows : (plane + 1) * rows, :] + (mask * scale) * (c * (1.0 / 3.0) + around * (1.0 / 9.0))

    def fine_around(field, y, center, edges=True):
        at = pl.multiple_of(y * 32, 32)
        total = field[pl.ds(at, 32), :] + field[pl.ds(at + 64, 32), :]
        low = jnp.broadcast_to(GX[0, pl.ds(y, 1), :], (32, 128)) if edges else 0.0
        high = jnp.broadcast_to(GX[1, pl.ds(y, 1), :], (32, 128)) if edges else 0.0
        total = total + jnp.where(first32 > 0, low, roll(center, 1, 0)) + jnp.where(last32 > 0, high, roll(center, -1, 0))
        total = total + (pick(center, index_low) * mask_low32 + pick(center, index_high) * mask_high32)
        return total + CGZ[pl.ds(pl.multiple_of((y >> 1) * 32, 32), 32), :]

    def restrict_fine(values, y):
        at = pl.multiple_of(y * 32, 32)
        T[pl.ds(at, 32), :] = values
        t = T[pl.ds(at, 16, stride=2), :] + T[pl.ds(at + 1, 16, stride=2), :]
        return pick(t + roll(t, -1, 1), index_in) * 0.125

    def double(ref, at, value):
        ref[pl.ds(at, value.shape[0], stride=2), :] = value
        ref[pl.ds(at + 1, value.shape[0], stride=2), :] = value

    def set_ghosts(inbox):
        GX[0, :, :] = pick(inbox[1, 0:32, :], index_g[0]) * tile(mask_g[0], 4) + CB[0:32, :]
        GX[1, :, :] = pick(inbox[0, 0:32, :], index_g[1]) * tile(mask_g[1], 4) + CB[32:64, :]
        FA[0:32, :] = pick(inbox[3, 0:32, :], index_g[2]) * tile(mask_g[2], 4) + CB[64:96, :]
        FA[33 * 32 : 34 * 32, :] = pick(inbox[2, 0:32, :], index_g[3]) * tile(mask_g[3], 4) + CB[96:128, :]

    def clear_y_ghosts():
        FA[0:32, :] = jnp.zeros((32, 128), F32)
        FA[33 * 32 : 34 * 32, :] = jnp.zeros((32, 128), F32)

    def outer(ref, d):
        if d == 0:
            return ref[pl.ds(2 * S0 + O0 - 1, 16, stride=S0), :]
        if d == 1:
            return ref[pl.ds(2 * S0 + O0 + 16, 16, stride=S0), :]
        plane = 1 if d == 2 else 18
        return ref[plane * S0 + O0 : plane * S0 + O0 + 16, :]

    def coarse_z(ref):
        for y in range(16):
            at = (y + 2) * S0 + O0
            double(CGZ, y * 32, pick(ref[at : at + 16, :], index_cz) * tile(mask_cz, 2))

    for cycle in range(CYCLES):
        if cycle == 0:
            CGZ[...] = jnp.zeros(CGZ.shape, F32)
        else:
            pack_faces(SA)
            SA[0, 32:48, :] = B0[pl.ds(2 * S0 + O0, 16, stride=S0), :]
            SA[1, 32:48, :] = B0[pl.ds(2 * S0 + O0 + 15, 16, stride=S0), :]
            SA[2, 32:48, :] = B0[2 * S0 + O0 : 2 * S0 + O0 + 16, :]
            SA[3, 32:48, :] = B0[17 * S0 + O0 : 17 * S0 + O0 + 16, :]
            wait_a = send_faces(SA, RA)
            coarse_z(B0)
            clear_y_ghosts()

            def first_sweep(y, _):
                at = pl.multiple_of(y * 32, 32)
                center = FA[pl.ds(at + 32, 32), :]
                around = fine_around(FA, y, center, False)
                FB[pl.ds(at + 32, 32), :] = keep32 * (
                    G[pl.ds(at, 32), :] + center * (1.0 / 3.0) + around * (1.0 / 9.0)
                )
                return 0

            lax.fori_loop(0, 32, first_sweep, 0, unroll=4)
            finish(wait_a)
            B0[pl.ds(2 * S0 + O0 + 16, 16, stride=S0), :] = RA[0, 32:48, :]
            B0[pl.ds(2 * S0 + O0 - 1, 16, stride=S0), :] = RA[1, 32:48, :]
            B0[18 * S0 + O0 : 18 * S0 + O0 + 16, :] = RA[2, 32:48, :]
            B0[1 * S0 + O0 : 1 * S0 + O0 + 16, :] = RA[3, 32:48, :]
            for d in range(4):
                double(CB, d * 32, pick(outer(B0, d), index_p) * tile(1.0 - mask_g[d], 2))
            set_ghosts(RA)

            ninth = keep32 * (1.0 / 9.0)
            FB[32:64, :] = FB[32:64, :] + ninth * FA[0:32, :]
            FB[32 * 32 : 33 * 32, :] = FB[32 * 32 : 33 * 32, :] + ninth * FA[33 * 32 : 34 * 32, :]
            for d, first in enumerate((32, 63)):
                face = pl.ds(first, 32, stride=32)
                FB[face, :] = FB[face, :] + ninth * GX[d, :, :]
            FA, FB = FB, FA
            pack_faces(SB.at[cycle])
            wait_b = send_faces(SB.at[cycle], RB.at[cycle])

        if cycle == 0:
            for y in range(16):
                at = (y + 2) * S0
                P0[at : at + S0, :] = BR[at : at + S0, :]
        else:
            for y in range(16):
                at = (y + 2) * S0
                c, around = neighbours(B0, y + 2, S0, 1)
                P0[at : at + S0, :] = BR[at : at + S0, :] - C0[at : at + S0, :] * (6.0 * c - around)

        clear_y_ghosts()

        def residual(y, _):
            def one(k):
                at = pl.multiple_of(k * 32, 32)
                center = FA[pl.ds(at + 32, 32), :]
                around = fine_around(FA, k, center, False)
                return BT[pl.ds(at, 32), :] * (9.0 * G[pl.ds(at, 32), :] - 6.0 * center + around)

            both = one(2 * y) + one(2 * y + 1)
            T[pl.ds(pl.multiple_of(y * 32, 32), 32), :] = both
            return 0

        lax.fori_loop(0, 16, residual, 0, unroll=2)
        finish(wait_b)
        set_ghosts(RB.at[cycle])
        T[0:32, :] = T[0:32, :] + BT[0:32, :] * FA[0:32, :]
        T[480:512, :] = T[480:512, :] + BT[31 * 32 : 32 * 32, :] * FA[33 * 32 : 34 * 32, :]
        for d, first in enumerate((0, 31)):
            face = pl.ds(first, 16, stride=32)
            T[face, :] = (
                T[face, :]
                + BT[pl.ds(first, 16, stride=64), :] * GX[d, pl.ds(0, 16, stride=2), :]
                + BT[pl.ds(first + 32, 16, stride=64), :] * GX[d, pl.ds(1, 16, stride=2), :]
            )
        for y in range(16):
            t = T[pl.ds(y * 32, 16, stride=2), :] + T[pl.ds(y * 32 + 1, 16, stride=2), :]
            means = pick(t + roll(t, -1, 1), index_in) * 0.125
            at = (y + 2) * S0 + O0
            P0[at : at + 16, :] = jnp.where(mask_in16 > 0, means, P0[at : at + 16, :]) * W0[at : at + 16, :]

        stage, corner = SC.at[cycle], SCC.at[cycle]
        for k in range(2):
            part = slice(k * 16, k * 16 + 16)
            stage[0, part, :] = P0[pl.ds(2 * S0 + O0 + k, 16, stride=S0), :]
            stage[1, part, :] = P0[pl.ds(2 * S0 + O0 + 14 + k, 16, stride=S0), :]
            stage[2, part, :] = P0[(2 + k) * S0 + O0 : (2 + k) * S0 + O0 + 16, :]
            stage[3, part, :] = P0[(16 + k) * S0 + O0 : (16 + k) * S0 + O0 + 16, :]
            for d in range(4):
                dx, dy = DIRS[4 + d]
                at = ((2 if dy < 0 else 16) + k) * S0 + O0 + (0 if dx < 0 else 14)
                corner[d, 2 * k : 2 * k + 2, :] = P0[at : at + 2, :]
        inbox, corners = RC.at[cycle], RCC.at[cycle]
        wait_c = start([(*DIRS[d], stage.at[d], inbox.at[d]) for d in range(4)])
        wait_cc = start([(*DIRS[4 + d], corner.at[d], corners.at[d]) for d in range(4)])

        def before(y, _):
            at = pl.multiple_of(y * 32, 32)
            center = FA[pl.ds(at + 32, 32), :]
            around = fine_around(FA, y, center)
            FB[pl.ds(at + 32, 32), :] = keep32 * (
                G[pl.ds(at, 32), :] + center * (1.0 / 3.0) + around * (1.0 / 9.0)
            )
            return 0

        lax.fori_loop(0, 32, before, 0, unroll=4)
        finish(wait_c)
        for k in range(2):
            part = slice(k * 16, k * 16 + 16)
            P0[pl.ds(2 * S0 + O0 + 16 + k, 16, stride=S0), :] = inbox[0, part, :]
            P0[pl.ds(2 * S0 + O0 - 2 + k, 16, stride=S0), :] = inbox[1, part, :]
            P0[(18 + k) * S0 + O0 : (18 + k) * S0 + O0 + 16, :] = inbox[2, part, :]
            P0[k * S0 + O0 : k * S0 + O0 + 16, :] = inbox[3, part, :]

        def left0(plane):
            c, around = neighbours(P0, plane, S0, 1)
            return C0[plane * S0 : (plane + 1) * S0, :] * (3.0 * c + around)

        for y in range(8):
            at = (y + 5) * S1 + O1
            P1[at : at + 8, :] = restrict0(left0, y) * W1[y * 8 : y * 8 + 8, :]
        wait_d = send_level1(P1, SD.at[cycle], RD.at[cycle])
        if cycle == 0:
            finish(wait_p)
            unpack_level1(C1, RP)
            for y in range(8):
                c = restrict1(lambda p: C1[p * S1 : (p + 1) * S1, :], y) * 0.25
                C2[y * 8 : y * 8 + 8, :] = c
                W2[y * 8 : y * 8 + 8, :] = jnp.where(c > 0, 1.0 / (9.0 * jnp.where(c > 0, c, 1.0)), 0.0)
            for y in range(2):
                c = restrict2(lambda p: C2[p * S2 : (p + 1) * S2, :], y) * 0.25
                W3[y * 4 : y * 4 + 4, :] = jnp.where(c > 0, 1.0 / (9.0 * jnp.where(c > 0, c, 1.0)), 0.0)
        finish(wait_cc)
        for k in range(2):
            for d in range(4):
                dx, dy = DIRS[4 + d]
                at = ((18 if dy < 0 else 0) + k) * S0 + (O0 + 16 if dx < 0 else O0 - 2)
                P0[at : at + 2, :] = corners[d, 2 * k : 2 * k + 2, :]
        finish(wait_d)
        unpack_level1(P1, RD.at[cycle])

        def left1(plane):
            c, around = neighbours(P1, plane, S1, 2)
            return C1[plane * S1 : (plane + 1) * S1, :] * (3.0 * c + around)

        for y in range(8):
            P2[y * 8 : y * 8 + 8, :] = restrict1(left1, y) * W2[y * 8 : y * 8 + 8, :]

        def left2(plane):
            c, around = neighbours(P2, plane, S2, 4)
            return C2[plane * S2 : (plane + 1) * S2, :] * (3.0 * c + around)

        mine = jnp.concatenate([restrict2(left2, y) for y in range(2)], axis=0) * W3[...]
        strip = SW.at[cycle]
        strip[...] = pick(mine, (lane8 & 15) * 8)
        wait_w = start([(0, k, strip, RW.at[cycle, 3 - k]) for k in REACH])
        finish(wait_w)
        joined = jnp.where((lane8 >> 4) == 3, strip[...], 0.0)
        for k in REACH:
            joined = jnp.where((lane8 >> 4) == 3 + k, RW[cycle, 3 + k, :, :], joined)
        SX[cycle, :, :] = joined
        wait_x = start([(k, 0, SX.at[cycle], RX.at[cycle, pl.ds((3 - k) * 8, 8)]) for k in REACH])
        RX[cycle, 24:32, :] = joined
        finish(wait_x)

        first = [[RX[cycle, pl.ds(y * 4 + 1 + x, 8, stride=8), :] for x in range(2)] for y in range(2)]
        col_x = gx + row8 - 3
        col_y = gy + (lane8 >> 4) - 3
        there = (col_x >= 0) & (col_x < nx) & (row8 < 7) & (col_y >= 0) & (col_y < ny) & (lane8 < 112)
        mask3 = jnp.where(there, 1.0, 0.0).astype(F32)
        e = first
        for sweep in range(SWEEPS - 1):
            new = [[None, None], [None, None]]
            for y in range(2):
                for x in range(2):
                    c, ex, ey = e[y][x], e[y][1 - x], e[1 - y][x]
                    around = ex + roll(ex, 1 if x == 0 else -1, 0) + ey + roll(ey, 16 if y == 0 else -16, 1)
                    around = around + jnp.where((lane8 & 15) > 0, roll(c, 1, 1), 0.0)
                    around = around + jnp.where((lane8 & 15) < 15, roll(c, -1, 1), 0.0)
                    new[y][x] = first[y][x] + mask3 * (c * (1.0 / 3.0) + around * (1.0 / 9.0))
            e = new

        from_one = jnp.where(row8 < 2, 2, 3)
        from_zero = jnp.where(row8 < 4, 3, 4)
        for k, (column, y) in enumerate(((2, 1), (3, 0), (3, 1), (4, 0))):
            lanes = column * 16 + (lane8 >> 3)
            zero, one = pick(e[y][0], lanes), pick(e[y][1], lanes)
            zero = jnp.take_along_axis(zero, from_zero, axis=0, mode="promise_in_bounds")
            one = jnp.take_along_axis(one, from_one, axis=0, mode="promise_in_bounds")
            up = jnp.where((row8 & 2) == 0, one, zero)
            for plane in (2 * k, 2 * k + 1):
                E2[plane * 8 : plane * 8 + 8, :] = P2[plane * 8 : plane * 8 + 8, :] + up
        for plane in range(1, 7):
            up = post(P2, E2, plane, S2, 4, rows2, plane_mask(plane - 2, 4, ny * 4))
            at = plane * S1
            double(U1, at + 4, up)
            for fine in (2 * plane + 1, 2 * plane + 2):
                E1[fine * S1 : (fine + 1) * S1, :] = P1[fine * S1 : (fine + 1) * S1, :] + U1[at : at + S1, :]
        for plane in range(4, 14):
            at = plane * S1
            U1[at : at + S1, :] = post(P1, E1, plane, S1, 2, rows1, plane_mask(plane - 5, 8, ny * 8))
            value = U1[at + 7 : at + 17, :]
            fine = 2 * (plane - 4)
            double(E0, fine * S0 + 2, value)
            up = E0[fine * S0 : (fine + 1) * S0, :]
            E0[(fine + 1) * S0 : (fine + 2) * S0, :] = up + P0[(fine + 1) * S0 : (fine + 2) * S0, :]
            E0[fine * S0 : (fine + 1) * S0, :] = up + P0[fine * S0 : (fine + 1) * S0, :]
        for plane in range(1, 19):
            at = plane * S0
            P0[at : at + S0, :] = post(P0, E0, plane, S0, 1, rows0, plane_mask(plane - 2, 16, ny * 16))
            B0[at : at + S0, :] = B0[at : at + S0, :] + P0[at : at + S0, :]

        for y in range(16):
            at = (y + 2) * S0 + O0
            double(PC, (y + 1) * 32, pick(P0[at : at + 16, :], index_p))
        coarse_z(P0)
        CB[0:16, :] = pick(outer(P0, 0), index_p)
        CB[16:32, :] = pick(outer(P0, 1), index_p)
        double(PC, 0, pick(outer(P0, 2), index_p))
        double(PC, 17 * 32, pick(outer(P0, 3), index_p))

        def last_sweep(y, _):
            at = pl.multiple_of(y * 32, 32)
            center = PC[pl.ds(at + 32, 32), :]
            low = jnp.broadcast_to(CB[pl.ds(y, 1), :], (32, 128))
            high = jnp.broadcast_to(CB[pl.ds(y + 16, 1), :], (32, 128))
            around = jnp.where(first32 > 0, low, roll(center, 1, 0)) + jnp.where(last32 > 0, high, roll(center, -1, 0))
            around = around + (pick(center, index_low) * mask_low32 + pick(center, index_high) * mask_high32)
            around = around + (CGZ[pl.ds(at, 32), :] + center)
            shared = center * (1.0 / 3.0) + around * (1.0 / 9.0)

            def one(k, beside):
                rows_k = pl.ds(pl.multiple_of(y * 64 + k * 32 + 32, 32), 32)
                new = FB[rows_k, :] + keep32 * (shared + PC[pl.ds(beside, 32), :] * (1.0 / 9.0))
                FA[rows_k, :] = new
                return new

            T[pl.ds(at, 32), :] = one(0, at) + one(1, pl.multiple_of(at + 64, 32))
            return 0

        lax.fori_loop(0, 16, last_sweep, 0, unroll=4)
        for y in range(16):
            t = T[pl.ds(y * 32, 16, stride=2), :] + T[pl.ds(y * 32 + 1, 16, stride=2), :]
            means = pick(t + roll(t, -1, 1), index_in) * 0.125
            at = (y + 2) * S0 + O0
            B0[at : at + 16, :] = jnp.where(mask_in16 > 0, means, B0[at : at + 16, :])

    def store_fine(j, _):
        planes = exchange_chunks([FA[pl.ds(pl.multiple_of((4 * j + k + 1) * 32, 32), 32), :] for k in range(4)])
        for s in range(4):
            fout_ref[0, 0, s, :, pl.ds(pl.multiple_of(j * 128, 128), 128)] = planes[s]
        return 0

    lax.fori_loop(0, 8, store_fine, 0)
    for y in range(16):
        at = (y + 2) * S0 + O0
        bout_ref[pl.ds(y, 16, stride=16), :] = B0[at : at + 16, :]
    for dx, dy, copy in pending:
        pl.when(inside(dx, dy))(lambda copy=copy: copy().wait_send())


def solution(mesh):
    nx, ny = mesh.shape["gx"], mesh.shape["gy"]

    def local(fine_rhs, fine_beta, base_rhs, base_beta, slot_site, ghost_list, box_count):
        vmem = pl.BlockSpec(memory_space=pltpu.VMEM)
        smem = pl.BlockSpec(memory_space=pltpu.SMEM)

        def rows(*shape):
            return pltpu.VMEM((*shape, 128), F32)

        fine, base = pl.pallas_call(
            lambda *refs: kernel(nx, ny, *refs),
            out_shape=(
                jax.ShapeDtypeStruct(fine_rhs.shape, F32),
                jax.ShapeDtypeStruct((256, 128), F32),
            ),
            in_specs=[smem] * 3 + [pl.BlockSpec(memory_space=pltpu.HBM)] * 4,
            out_specs=(vmem, vmem),
            scratch_shapes=[
                pltpu.VMEM(fine_rhs.shape[2:], F32),
                pltpu.VMEM(fine_rhs.shape[2:], F32),
                rows(256),
                rows(256),
                pltpu.SemaphoreType.DMA((4,)),
                rows(34 * 32),
                rows(34 * 32),
                rows(32 * 32),
                rows(32 * 32),
                rows(18 * 32),
                rows(16 * 32),
                rows(16 * 32),
                rows(2, 32),
                rows(4 * 32),
                rows(20 * S0),
                rows(20 * S0),
                rows(20 * S0),
                rows(20 * S0),
                rows(20 * S0),
                rows(20 * S0),
                rows(8 * S0),
                rows(18 * S1),
                rows(64),
                rows(18 * S1),
                rows(18 * S1),
                rows(18 * S1),
                rows(8 * S1),
                rows(64),
                rows(64),
                rows(64),
                rows(64),
                rows(16),
                rows(8),
                rows(4, 24),
                rows(8, 24),
                rows(4, 48),
                rows(4, 48),
                rows(2, 4, 32),
                rows(2, 4, 32),
                rows(2, 4, 32),
                rows(2, 4, 8),
                rows(2, 4, 32),
                rows(2, 4, 8),
                rows(2, 4, 24),
                rows(2, 8, 24),
                rows(2, 8),
                rows(2, 7, 8),
                rows(2, 8),
                rows(2, 64),
                pltpu.SemaphoreType.DMA((SEM_COUNT,)),
                pltpu.SemaphoreType.DMA((SEM_COUNT,)),
            ],
            compiler_params=pltpu.CompilerParams(
                collective_id=0, has_side_effects=True, vmem_limit_bytes=48_000_000
            ),
            name="vcycles",
        )(
            pltpu.with_memory_space_constraint(slot_site, pltpu.HBM),
            pltpu.with_memory_space_constraint(ghost_list, pltpu.HBM),
            box_count,
            pltpu.with_memory_space_constraint(fine_rhs, pltpu.HBM),
            pltpu.with_memory_space_constraint(fine_beta, pltpu.HBM),
            pltpu.with_memory_space_constraint(base_rhs.reshape(256, 128), pltpu.HBM),
            pltpu.with_memory_space_constraint(base_beta.reshape(256, 128), pltpu.HBM),
        )
        return fine, base.reshape(16, 16, 128)

    return jax.shard_map(
        local,
        mesh=mesh,
        in_specs=(
            P("gx", "gy", None, None, None),
            P("gx", "gy", None, None, None),
            P("gx", "gy", None),
            P("gx", "gy", None),
            P("gx", "gy", None),
            P("gx", "gy", None, None),
            P("gx", "gy"),
        ),
        out_specs=(P("gx", "gy", None, None, None), P("gx", "gy", None)),
        check_vma=False,
    )
```
